128 devices in a mesh: aa: 8 (over x, core), ba: 16 (over y, z).
Axes of the slice: x: 4, y: 4, z: 4, core: 2. Of those that a mesh axis runs over, the one named last changes fastest.
Arguments:
- rotation_harmonics: bfloat16 [32, 2, 819840], P('ba', None, 'aa'), may hold values from -2048 to 2048
- dilation_harmonics: bfloat16 [32, 2, 819840], P('ba', None, 'aa'), may hold values from -2048 to 2048
- thermal_harmonics: bfloat16 [32, 2, 819840], P('ba', None, 'aa'), may hold values from -3 to 3
- associated_polynomials: bfloat16 [48, 819840], P(None, 'aa'), may hold values from -0.0068359375 to 0.0068359375
- harmonic_order_list: int32 [8, 160], replicated, may hold values from 0 to 1279, as said below
- meridian_counts: int32 [96], replicated, may hold values from 20 to 5136, as said below
- latitude_limits: int32 [9], replicated, may hold values from 0 to 96, as said below
Outputs:
- zonal_velocity_mesh: float32 [32, 128, 6144], P(None, 'aa', 'ba')
- meridional_velocity_mesh: float32 [32, 128, 6144], P(None, 'aa', 'ba')
- temp_grid: float32 [32, 128, 6144], P(None, 'aa', 'ba')
The draws below stay inside these ranges and needn't reach their ends.
Inputs may be any that keep to these rules, and one draw needn't show every extreme that they name: `harmonic_order_list`: row a lists the wavenumbers of index a of aa as 80 pairs: entry 2j is some p below 640 and entry 2j+1 is 1279-p; every wavenumber stands once in the whole array. `meridian_counts`: window latitudes run from north to south: the first 48 have 20 + 4 j points for distinct rising j below 1280, the last 48 repeat these counts in reverse order, and the largest count is 5136. `latitude_limits`: the first entry is 0 and the last 96; entries rise; each band holds 1 to 16 latitudes and one band holds exactly 16.
All inputs are finite; a program needn't handle non-finite values.
Results may differ from the reference program's by a relative error of at most 0.0047.
Values may be sent and summed in bfloat16 or wider, within the bound.
No kernel may reach another device: no remote copies, remote signals or barrier semaphores. Data moves between devices by JAX's collectives and lax.ppermute only.
A program may use at most 192 MiB of HBM per device.

```python
import math
import jax
import jax.numpy as jnp
from jax import lax

MW = 1280
HALF_LAT = 1280
HEIGHT_COUNT = 32
LAT_DEV = 12
BAND_MAX = 16
LATW = 96
LATH = 48
MDEV = 160
HARMONIC_COUNT = 819840
PIECE = 384
LONP = 6144
N_AA = 8


def pair_table(key):
    order = jax.random.permutation(jax.random.fold_in(key, 11), MW // 2).astype(jnp.int32)
    lower = order.reshape(N_AA, MDEV // 2)
    return jnp.stack([lower, MW - 1 - lower], axis=-1).reshape(N_AA, MDEV)


def packed_degree(key):
    table = pair_table(key)
    lower = table[:, 0::2]
    position = jnp.arange(MW + 1, dtype=jnp.int32)
    first_seg = position[None, None, :] < (MW - lower)[:, :, None]
    degree = jnp.where(first_seg, lower[:, :, None] + position[None, None, :], position[None, None, :] - 1)
    return degree.reshape(HARMONIC_COUNT)


def spectral_field(key, salt):
    degree = packed_degree(key).astype(jnp.float32) + 1.0
    inner = jax.random.fold_in(key, salt)
    first_key = jax.random.fold_in(inner, 0)
    noise = jnp.clip(jax.random.normal(first_key, (HEIGHT_COUNT, 2, HARMONIC_COUNT), jnp.float32), -4.0, 4.0)
    return (0.4 * degree[None, None, :] * noise).astype(jnp.bfloat16)


def draw_rotation_harmonics(key, part):
    return spectral_field(key, 21)


def draw_dilation_harmonics(key, part):
    return spectral_field(key, 22)


def draw_harmonic_order_list(key, part):
    return pair_table(key)


def draw_meridian_counts(key, part):
    stride = HALF_LAT // LATH
    offsets = jax.random.randint(jax.random.fold_in(key, 31), (LATH,), 0, stride, dtype=jnp.int32)
    index = jnp.arange(LATH, dtype=jnp.int32)
    rows = jnp.where(index == LATH - 1, HALF_LAT - 1, index * stride + offsets)
    northern = 20 + 4 * rows
    return jnp.concatenate([northern, northern[::-1]]).astype(jnp.int32)


def draw_latitude_limits(key, part):
    first_key, second_key = jax.random.split(jax.random.fold_in(key, 41))
    heavy = jax.random.randint(first_key, (), 0, N_AA, dtype=jnp.int32)
    light = (heavy + 1 + jax.random.randint(second_key, (), 0, N_AA - 1, dtype=jnp.int32)) % N_AA
    extra = BAND_MAX - LAT_DEV
    index = jnp.arange(N_AA, dtype=jnp.int32)
    counts = LAT_DEV + extra * (index == heavy).astype(jnp.int32) - extra * (index == light).astype(jnp.int32)
    return jnp.concatenate([jnp.zeros((1,), jnp.int32), jnp.cumsum(counts).astype(jnp.int32)])


def levels(key, extent, cuts, smallest, largest):
    gain = 1.0
    for dim, shards_of in cuts:
        steps = jax.random.uniform(jax.random.fold_in(jax.random.fold_in(key, 6), dim), (shards_of,), jnp.float32, smallest / len(cuts), largest / len(cuts))
        gain = gain * jnp.repeat(jnp.exp(steps), extent[dim] // shards_of).reshape((-1,) + (1,) * (len(extent) - 1 - dim))
    return gain


def scatter_about(own_key, extent, spread, reach, shards=(), kind=jnp.bfloat16):
    drawn = jax.random.normal(own_key, extent, jnp.float32) * spread
    if len(shards) > 0:
        drawn = levels(own_key, extent, shards, -0.22, 0.18) * drawn
    return jnp.clip(drawn, min=-reach, max=reach).astype(kind)


def setup_inputs(seed: int = 0) -> dict:
    key_of = jax.random.split(jax.random.key(seed), 8)
    return {
        "rotation_harmonics": draw_rotation_harmonics(jax.random.fold_in(key_of[7], 71), 0),
        "dilation_harmonics": draw_dilation_harmonics(jax.random.fold_in(key_of[7], 71), 0),
        "thermal_harmonics": scatter_about(key_of[2], (HEIGHT_COUNT, 2, HARMONIC_COUNT), 0.5, 3.0, ((0, 16), (2, 8))),
        "associated_polynomials": scatter_about(key_of[3], (LATH, HARMONIC_COUNT), (MW * MW // 2) ** -0.5, 0.0068359375, ((1, 8),)),
        "harmonic_order_list": draw_harmonic_order_list(jax.random.fold_in(key_of[7], 71), 0),
        "meridian_counts": draw_meridian_counts(jax.random.fold_in(key_of[7], 71), 0),
        "latitude_limits": draw_latitude_limits(jax.random.fold_in(key_of[7], 71), 0),
    }


full_turn = 2.0 * math.pi

def pair_layout(lower_waves):
    position = jnp.arange(MW + 1, dtype=jnp.int32)
    first_seg = position[None, :] < (MW - lower_waves)[:, None]
    wavenum = jnp.where(first_seg, lower_waves[:, None], MW - 1 - lower_waves[:, None])
    degree = jnp.where(first_seg, lower_waves[:, None] + position[None, :], position[None, :] - 1)
    return (first_seg, wavenum.astype(jnp.int32), degree.astype(jnp.int32))

def shift_down(values):
    return jnp.concatenate([jnp.zeros_like(values[..., :1]), values[..., :-1]], axis=-1)

def shift_up(values):
    return jnp.concatenate([values[..., 1:], jnp.zeros_like(values[..., :1])], axis=-1)

def times_i(values):
    return jnp.stack([-values[:, 1], values[:, 0]], axis=1)

def spectral_winds(curl_field, spread_field, first_seg, wavenum, degree):
    order_m = wavenum.astype(jnp.float32)
    order_n = degree.astype(jnp.float32)
    denom = jnp.maximum(order_n * (order_n + 1.0), 1.0)
    stream = jnp.where(degree > 0, -curl_field.astype(jnp.float32) / denom, 0.0)
    potential = jnp.where(degree > 0, -spread_field.astype(jnp.float32) / denom, 0.0)
    coupling = jnp.sqrt(jnp.maximum((order_n * order_n - order_m * order_m) / (4.0 * order_n * order_n - 1.0), 0.0))
    seg_flag = first_seg.astype(jnp.int32)
    same_seg = (seg_flag == shift_up(seg_flag)).astype(jnp.float32)
    coupling_up = shift_up(coupling) * same_seg
    lower = (order_n - 1.0) * coupling
    upper = (order_n + 2.0) * coupling_up
    zonal_velocity_mesh = lower * shift_down(stream) - upper * shift_up(stream) + order_m * times_i(potential)
    meridional_velocity_mesh = -lower * shift_down(potential) + upper * shift_up(potential) + order_m * times_i(stream)
    return (zonal_velocity_mesh.astype(jnp.bfloat16), meridional_velocity_mesh.astype(jnp.bfloat16))

def legendre_columns(spectral_inputs, first_seg, wavenum, degree):
    spectra_t = jnp.transpose(spectral_inputs, (3, 4, 2, 0, 1))
    even_parity = (degree - wavenum) % 2 == 0
    segment = jnp.stack([first_seg, jnp.logical_not(first_seg)], axis=-1)
    parity = jnp.stack([even_parity, jnp.logical_not(even_parity)], axis=-1)
    selector = jnp.logical_and(segment[:, :, :, None], parity[:, :, None, :]).astype(jnp.bfloat16)
    grid_column_set = spectra_t[:, :, None, None] * selector[:, :, :, :, None, None, None]
    return grid_column_set.reshape(grid_column_set.shape[0], grid_column_set.shape[1], -1)

def fold_hemispheres(transform_output, level_count):
    shaped = transform_output.reshape(transform_output.shape[0], transform_output.shape[1], 2, 2, 2, 3, level_count)
    northern = shaped[:, :, :, 0] + shaped[:, :, :, 1]
    southern = shaped[:, :, :, 0] - shaped[:, :, :, 1]
    return jnp.concatenate([northern, southern[:, ::-1]], axis=1).astype(jnp.bfloat16)

def trig_table(wave_table, longitudes, lon_count, occupied):
    residue = wave_table[:, :, None] * longitudes[None, None, :] % lon_count
    angles = residue.astype(jnp.float32) * full_turn / lon_count.astype(jnp.float32)
    active = occupied & (longitudes[None, None, :] < lon_count) & (wave_table[:, :, None] <= (lon_count - 1) // 2)
    weights = (jnp.where(wave_table == 0, 1.0, 2.0)[:, :, None] * active).astype(jnp.bfloat16)
    cosine = jnp.cos(angles).astype(jnp.bfloat16) * weights
    sine_part = (-jnp.sin(angles)).astype(jnp.bfloat16) * weights
    return jnp.stack([cosine, sine_part], axis=1)

def reference(rotation_harmonics, dilation_harmonics, thermal_harmonics, associated_polynomials, harmonic_order_list, meridian_counts, latitude_limits):
    pair_total = MW // 2
    block = 16
    blocks = pair_total // block
    width = MW + 1

    def partition_matrix(field):
        return jnp.transpose(field.reshape(HEIGHT_COUNT, 2, blocks, block, width), (2, 0, 1, 3, 4))
    partition_lookup = jnp.transpose(associated_polynomials.reshape(LATH, blocks, block, width), (1, 0, 2, 3))
    reduce_each_strip = harmonic_order_list[:, 0::2].reshape(blocks, block)

    def solitary_partition(inputs):
        curl_block, spread_block, heat_block, block_of_table, lower_block = inputs
        first_seg, wavenum, degree = pair_layout(lower_block)
        zonal_velocity_mesh, meridional_velocity_mesh = spectral_winds(curl_block, spread_block, first_seg, wavenum, degree)
        spectral_inputs = jnp.stack([zonal_velocity_mesh, meridional_velocity_mesh, heat_block], axis=0)
        grid_column_set = legendre_columns(spectral_inputs, first_seg, wavenum, degree)
        transform_output = jnp.einsum('ptf,tfq->tpq', block_of_table.astype(jnp.float32), grid_column_set.astype(jnp.float32))
        return fold_hemispheres(transform_output, HEIGHT_COUNT)
    azimuthal_harmonics = lax.map(solitary_partition, (partition_matrix(rotation_harmonics), partition_matrix(dilation_harmonics), partition_matrix(thermal_harmonics), partition_lookup, reduce_each_strip))
    azimuthal_harmonics = azimuthal_harmonics.reshape(pair_total, LATW, 2, 2, 3, HEIGHT_COUNT)
    azimuthal_harmonics = jnp.transpose(azimuthal_harmonics, (1, 3, 0, 2, 4, 5)).reshape(LATW, 2 * MW, 3 * HEIGHT_COUNT)
    column = jnp.arange(LONP, dtype=jnp.int32)
    longitudes = column % PIECE * (LONP // PIECE) + column // PIECE

    def one_latitude(inputs):
        data, lon_count = inputs
        table = trig_table(harmonic_order_list, longitudes, lon_count, True)
        table = jnp.transpose(table, (1, 0, 2, 3)).reshape(2 * MW, LONP)
        return jnp.dot(data.T, table, preferred_element_type=jnp.float32)
    values = lax.map(one_latitude, (azimuthal_harmonics, meridian_counts))
    rows = jnp.arange(N_AA * BAND_MAX, dtype=jnp.int32)
    band = rows // BAND_MAX
    latitude = latitude_limits[band] + rows % BAND_MAX
    occupied = latitude < latitude_limits[band + 1]
    picked = values[jnp.minimum(latitude, LATW - 1)] * occupied[:, None, None].astype(jnp.float32)
    picked = jnp.transpose(picked.reshape(N_AA * BAND_MAX, 3, HEIGHT_COUNT, LONP), (1, 2, 0, 3))
    return (picked[0], picked[1], picked[2])
```

```python
import functools
import math

import jax
import jax.numpy as jnp
from jax import lax
from jax.experimental import pallas as pl
from jax.experimental.pallas import tpu as pltpu
from jax.sharding import PartitionSpec as P

MW = 1280
WIDTH = MW + 1
PAIRS = 80
GROUP = 8
STEPS = PAIRS // GROUP
MAIN = GROUP * MW
WIN = 1408
LATH = 48
BAND_MAX = 16
PIECES = 16
PIECE = 384
LEVELS = 32
KM = 64
KR = PAIRS - KM
KALL = 2 * PAIRS
F32 = jnp.float32
BF16 = jnp.bfloat16
NT = (((1,), (1,)), ((), ()))


def wind_legendre_kernel(
    orders,
    limits,
    where_am_i,
    rot,
    rot_x,
    dil,
    dil_x,
    tmp,
    tmp_x,
    pol,
    pol_x,
    out,
    fields,
    heat,
    table,
    coef_a,
    coef_b,
    coef_c,
    north,
    south,
    tiles,
):
    step = pl.program_id(0)
    me = where_am_i[0]
    live = 102480 - (step + 1) * MAIN

    def edge(ref):
        lane = lax.broadcasted_iota(jnp.int32, (2, 128), 1)
        return [jnp.where(lane < live, ref[lv].astype(F32), 0.0).astype(BF16) for lv in range(2)]

    for src, (ref, ref_x) in enumerate(((rot, rot_x), (dil, dil_x))):
        tail = edge(ref_x)
        for lv in range(2):
            row = src * 4 + lv * 2
            fields[row : row + 2, 0:MAIN] = ref[lv]
            fields[row : row + 2, MAIN : MAIN + 128] = tail[lv]
    tail = edge(tmp_x)
    for copy in range(4):
        for lv in range(2):
            row = copy * 4 + lv * 2
            heat[row : row + 2, 0:MAIN] = tmp[lv]
            heat[row : row + 2, MAIN : MAIN + 128] = tail[lv]
    table[:, 0:MAIN] = pol[...]
    lane48 = lax.broadcasted_iota(jnp.int32, (LATH, 128), 1)
    table[:, MAIN : MAIN + 128] = jnp.where(lane48 < live, pol_x[...].astype(F32), 0.0).astype(BF16)

    lane = lax.broadcasted_iota(jnp.int32, (GROUP, WIN), 1)
    sub = lax.broadcasted_iota(jnp.int32, (GROUP, WIN), 0)
    low = [orders[me, 2 * (step * GROUP + s)] for s in range(GROUP)]
    sub1 = lax.broadcasted_iota(jnp.int32, (GROUP, 128), 0)
    lower1 = jnp.zeros((GROUP, 128), jnp.int32)
    for s in range(GROUP):
        lower1 = jnp.where(sub1 == s, low[s], lower1)
    lower = jnp.concatenate([lower1] * (WIN // 128), axis=1)
    pos = lane - sub - step * GROUP
    valid = (pos >= 0) & (pos < WIDTH)
    first = pos < MW - lower
    wave = jnp.where(first, lower, MW - 1 - lower).astype(F32)
    deg = jnp.where(first, lower + pos, pos - 1).astype(F32)
    usable = valid & (deg > 0.5)
    deg = jnp.where(usable, deg, 1.0)
    square = deg * deg
    eps_over_n = jnp.sqrt(
        jnp.maximum((deg - wave) * (deg + wave), 0.0) / ((4.0 * square - 1.0) * square)
    )
    eps_over_n = jnp.where(usable, eps_over_n, 0.0)
    coef_a[...] = jnp.where(deg > 1.5, eps_over_n, 0.0)
    coef_b[...] = pltpu.roll(eps_over_n, WIN - 1, 1)
    coef_c[...] = jnp.where(usable, wave / (square + deg), 0.0)

    early = step < KM // GROUP
    base = jnp.where(early, step * GROUP, 2 * KM + (step - KM // GROUP) * GROUP)
    seg_off = jnp.where(early, KM, KR)

    half_row = lax.broadcasted_iota(jnp.int32, (GROUP, WIN), 0) // 4
    lane_par = lane & 1
    for s in range(GROUP):
        lo = s * MW
        x = fields[:, lo : lo + WIN].astype(F32)
        a = coef_a[pl.ds(s, GROUP, stride=0), :]
        b = coef_b[pl.ds(s, GROUP, stride=0), :]
        c = coef_c[pl.ds(s, GROUP, stride=0), :]
        w = b * pltpu.roll(x, WIN - 1, 1) - a * pltpu.roll(x, 1, 1)
        cx = c * x
        j = step * GROUP + s
        cut = MW - low[s] + j
        in0 = (lane >= j) & (lane < cut)
        in1 = (lane >= cut) & (lane < j + WIDTH)
        par0 = (lane_par ^ (j & 1)) == 0
        par1 = (lane_par ^ ((j + low[s]) & 1)) == 0
        masks = [in0 & par0, in0 & ~par0, in1 & par1, in1 & ~par1]
        rows = []
        for mask in masks:
            rows.append(jnp.where(mask, w, 0.0))
            rows.append(jnp.where(mask, cx, 0.0))
        h = heat[:, lo : lo + WIN].astype(F32)
        top = jnp.where(half_row == 0, masks[0].astype(F32), masks[1].astype(F32))
        bottom = jnp.where(half_row == 0, masks[2].astype(F32), masks[3].astype(F32))
        rows.append(h[0:8] * top)
        rows.append(h[8:16] * bottom)
        data = jnp.concatenate(rows, axis=0).astype(BF16)
        res = lax.dot_general(data, table[:, lo : lo + WIN], NT, preferred_element_type=F32)
        for seg in range(2):
            at = base + s + seg * seg_off
            for part in range(2):
                even = res[seg * 32 + part * 8 : seg * 32 + part * 8 + 8]
                odd = res[seg * 32 + 16 + part * 8 : seg * 32 + 16 + part * 8 + 8]
                north[pl.ds(part * 8 * KALL + at, 8, stride=KALL), :] = even + odd
                south[pl.ds(part * 8 * KALL + at, 8, stride=KALL), :] = even - odd
            both = res[64 + seg * 8 : 72 + seg * 8]
            flip = pltpu.roll(both, 4, 0)
            north[pl.ds(16 * KALL + at, 4, stride=KALL), :] = (both + flip)[0:4]
            south[pl.ds(16 * KALL + at, 4, stride=KALL), :] = (both - flip)[0:4]

    @pl.when(step == STEPS - 1)
    def _():
        dest = lax.broadcasted_iota(jnp.int32, (128, LATH), 0)
        column = lax.broadcasted_iota(jnp.int32, (128, LATH), 1)
        lat = dest % BAND_MAX
        for band in range(8):
            lat = lat + jnp.where(dest // BAND_MAX == band, limits[band], 0)
        pick_n = (lat == column).astype(F32).astype(BF16)
        pick_s = (2 * LATH - 1 - lat == column).astype(F32).astype(BF16)

        def rows_of(ref, part, lv, fld, start, size):
            def at(row):
                return ref[row * KALL + start : row * KALL + start + size, :]

            if fld == 2:
                return at(16 + lv * 2 + part)
            w = at((4 if fld == 1 else 0) + lv * 2 + part)
            cx = at(8 + (0 if fld == 1 else 4) + lv * 2 + 1 - part)
            w = -w if fld == 1 else w
            return w + cx if part == 0 else w - cx

        def select(rows_n, rows_s, row):
            val = lax.dot_general(pick_n, rows_n.astype(BF16), NT, preferred_element_type=F32)
            val = val + lax.dot_general(pick_s, rows_s.astype(BF16), NT, preferred_element_type=F32)
            for block in range(16):
                tiles[pl.ds(row + 128 * block, 8, stride=16), :] = val[8 * block : 8 * block + 8]

        for part in range(2):
            for lv in range(2):
                for fld in range(3):
                    select(
                        rows_of(north, part, lv, fld, 0, 2 * KM),
                        rows_of(south, part, lv, fld, 0, 2 * KM),
                        part * 6 + lv * 3 + fld,
                    )
        for fld in range(3):
            both = []
            for ref in (north, south):
                both.append(
                    jnp.concatenate(
                        [
                            rows_of(ref, q // 2, q % 2, fld, 2 * KM, 2 * KR)
                            for q in range(4)
                        ],
                        axis=0,
                    )
                )
            select(both[0], both[1], 12 + fld)
        for block in range(16):
            tiles[pl.ds(15 + 128 * block, 8, stride=16), :] = jnp.zeros((8, 128), F32)
        for block in range(16):
            part = tiles[128 * block : 128 * block + 128, :]
            out[8 * block : 8 * block + 8] = part.reshape(8, 16, 128).astype(BF16)


def wind_legendre(rot, dil, tmp, pol, orders, limits, me):
    def smem(shape):
        return pl.BlockSpec(shape, lambda i: (0,) * len(shape), memory_space=pltpu.SMEM)

    main = pl.BlockSpec((2, 2, MAIN), lambda i: (0, 0, i))
    tail = pl.BlockSpec((2, 2, 128), lambda i: (0, 0, (i + 1) * (MAIN // 128)))
    return pl.pallas_call(
        wind_legendre_kernel,
        grid=(STEPS,),
        in_specs=[
            smem((8, 160)),
            smem((9,)),
            smem((1,)),
            main,
            tail,
            main,
            tail,
            main,
            tail,
            pl.BlockSpec((LATH, MAIN), lambda i: (0, i)),
            pl.BlockSpec((LATH, 128), lambda i: (0, (i + 1) * (MAIN // 128))),
        ],
        out_specs=pl.BlockSpec((128, 16, 128), lambda i: (0, 0, 0)),
        out_shape=jax.ShapeDtypeStruct((128, 16, 128), BF16),
        scratch_shapes=[
            pltpu.VMEM((8, MAIN + 128), BF16),
            pltpu.VMEM((16, MAIN + 128), BF16),
            pltpu.VMEM((LATH, MAIN + 128), BF16),
            pltpu.VMEM((GROUP, WIN), F32),
            pltpu.VMEM((GROUP, WIN), F32),
            pltpu.VMEM((GROUP, WIN), F32),
            pltpu.VMEM((20 * KALL, LATH), F32),
            pltpu.VMEM((20 * KALL, LATH), F32),
            pltpu.VMEM((2048, 128), F32),
        ],
        compiler_params=pltpu.CompilerParams(vmem_limit_bytes=40 * 1024 * 1024),
        name="wind_legendre",
    )(orders, limits, me, rot, rot, dil, dil, tmp, tmp, pol, pol)


def cos_sin_turns(turns):
    z = turns * (math.pi / 2.0)
    y = z * z
    sin = z * (1.0 + y * (-1 / 6 + y * (1 / 120 + y * (-1 / 5040 + y * (1 / 362880)))))
    cos = 1.0 + y * (-1 / 2 + y * (1 / 24 + y * (-1 / 720 + y * (1 / 40320 + y * (-1 / 3628800)))))
    s2 = 2.0 * sin * cos
    c2 = 1.0 - 2.0 * sin * sin
    return 1.0 - 2.0 * s2 * s2, 2.0 * s2 * c2


def fraction_of_turn(product, count, inverse):
    r = product - jnp.floor(product * inverse + 0.5) * count
    return r * inverse


def table_kernel(count, wave, table, twist_c, twist_s, weight):
    k = count[0].astype(F32)
    k_lane = jnp.maximum(jnp.full((8, 128), k, F32), 1.0)
    inverse = 1.0 / k_lane
    k1, inv1 = k_lane[0:1, 0:1], inverse[0:1, 0:1]
    m_row = wave[...].astype(F32)
    for q in range(2):
        piece = (lax.broadcasted_iota(jnp.int32, (8, MW), 0) + 8 * q).astype(F32)
        cos, sin = cos_sin_turns(fraction_of_turn(piece * m_row, k1, inv1))
        for row in range(8):
            twist_c[8 * q + row] = cos[row : row + 1]
            twist_s[8 * q + row] = sin[row : row + 1]
    top = jnp.full((8, MW), (count[0] - 1) // 2, jnp.int32)
    m8 = jnp.broadcast_to(wave[...], (8, MW))
    w = jnp.where(m8 == 0, 1.0, 2.0)
    weight[...] = jnp.where(m8 <= top, w, 0.0)
    for q in range(MW // 128):
        chunk = jnp.broadcast_to(m_row[:, 128 * q : 128 * q + 128], (128, 128))
        column = jnp.transpose(chunk, (1, 0))
        for c in range(PIECE // 128):
            x = ((lax.broadcasted_iota(jnp.int32, (128, 128), 1) + 128 * c) * PIECES).astype(F32)
            cos, sin = cos_sin_turns(fraction_of_turn(x * column, k1, inv1))
            table[128 * q : 128 * q + 128, 128 * c : 128 * c + 128] = cos.astype(BF16)
            table[MW + 128 * q : MW + 128 * q + 128, 128 * c : 128 * c + 128] = (-sin).astype(BF16)


def make_table(count, wave):
    return pl.pallas_call(
        table_kernel,
        in_specs=[pl.BlockSpec(memory_space=pltpu.SMEM), pl.BlockSpec(memory_space=pltpu.VMEM)],
        out_specs=[pl.BlockSpec(memory_space=pltpu.VMEM)] * 4,
        out_shape=[
            jax.ShapeDtypeStruct((2 * MW, PIECE), BF16),
            jax.ShapeDtypeStruct((PIECES, 1, MW), F32),
            jax.ShapeDtypeStruct((PIECES, 1, MW), F32),
            jax.ShapeDtypeStruct((8, MW), F32),
        ],
        compiler_params=pltpu.CompilerParams(vmem_limit_bytes=32 * 1024 * 1024),
        cost_estimate=pl.CostEstimate(flops=50_000_000, transcendentals=0, bytes_accessed=4_000_000),
        name="trig_table",
    )(count, wave)


PSTEP = 4


def grid_kernel(count, data, table, twist_c, twist_s, weight, out, f_re, f_im, twisted):
    step = pl.program_id(0)

    @pl.when(step == 0)
    def _():
        row = lax.broadcasted_iota(jnp.int32, (192, 256), 0)
        col = lax.broadcasted_iota(jnp.int32, (192, 256), 1)
        pick_main = (col == (row % 16) * 16 + row // 16).astype(F32).astype(BF16)
        pick_rest = (col == (row % 16) * 16 + 12 + (row // 16) % 3).astype(F32).astype(BF16)
        lane = lax.broadcasted_iota(jnp.int32, (48, 128), 1) // 32
        rest = [[jnp.zeros((48, 128), F32) for _ in range(2)] for _ in range(4)]
        for a in range(8):
            x = data[16 * a : 16 * a + 16].reshape(256, 128)
            lanes = slice(128 * a, 128 * a + 128)
            w = weight[0:1, lanes]
            main = jnp.dot(pick_main, x, preferred_element_type=F32)
            f_re[:, lanes] = main[0:96] * w
            f_im[:, lanes] = main[96:192] * w
            more = jnp.dot(pick_rest, x, preferred_element_type=F32)
            for q in range(4):
                piece = more[48 * q : 48 * q + 48]
                shift = (32 * (a % 4) - 32 * q) % 128
                if shift:
                    piece = pltpu.roll(piece, shift, 1)
                rest[q][a // 4] = jnp.where(lane == a % 4, piece, rest[q][a // 4])
        for half in range(2):
            lanes = slice(1024 + 128 * half, 1152 + 128 * half)
            w = weight[0:1, lanes]
            f_re[0:48, lanes] = rest[0][half] * w
            f_re[48:96, lanes] = rest[1][half] * w
            f_im[0:48, lanes] = rest[2][half] * w
            f_im[48:96, lanes] = rest[3][half] * w

    for u in range(PSTEP):
        piece = step * PSTEP + u
        for chunk in range(MW // 128):
            lanes = slice(128 * chunk, 128 * chunk + 128)
            cos = twist_c[piece, :, lanes]
            sin = twist_s[piece, :, lanes]
            re, im = f_re[:, lanes], f_im[:, lanes]
            twisted[96 * u : 96 * u + 96, lanes] = (re * cos - im * sin).astype(BF16)
            twisted[96 * u : 96 * u + 96, MW + 128 * chunk : MW + 128 * chunk + 128] = (
                re * sin + im * cos
            ).astype(BF16)
    res = jnp.dot(twisted[...], table[...], preferred_element_type=F32)
    lon = lax.broadcasted_iota(jnp.int32, (96, PIECE), 1) * PIECES + step * PSTEP
    for u in range(PSTEP):
        keep = lon + u < count[0]
        out[u] = jnp.where(keep, res[96 * u : 96 * u + 96], 0.0).astype(BF16)


def make_grid(count, data, tables):
    def whole(shape):
        return pl.BlockSpec(shape, lambda i: (0,) * len(shape))

    return pl.pallas_call(
        grid_kernel,
        grid=(PIECES // PSTEP,),
        in_specs=[
            pl.BlockSpec((1,), lambda i: (0,), memory_space=pltpu.SMEM),
            whole((128, 16, 128)),
            whole((2 * MW, PIECE)),
            whole((PIECES, 1, MW)),
            whole((PIECES, 1, MW)),
            whole((8, MW)),
        ],
        out_specs=pl.BlockSpec((PSTEP, 96, PIECE), lambda i: (i, 0, 0)),
        out_shape=jax.ShapeDtypeStruct((PIECES, 96, PIECE), BF16),
        scratch_shapes=[
            pltpu.VMEM((96, MW), F32),
            pltpu.VMEM((96, MW), F32),
            pltpu.VMEM((96 * PSTEP, 2 * MW), BF16),
        ],
        compiler_params=pltpu.CompilerParams(vmem_limit_bytes=48 * 1024 * 1024),
        name="grid_product",
    )(count, data, *tables)


def wave_row(orders):
    lower = orders[:, 0::2]
    both = jnp.stack([lower, MW - 1 - lower], axis=1)
    return jnp.concatenate([both[:, :, :KM].reshape(1, -1), both[:, :, KM:].reshape(1, -1)], axis=1)


def per_device(rot, dil, tmp, pol, orders, counts, limits):
    band = lax.axis_index("aa").astype(jnp.int32)
    slot = lax.axis_index("ba").astype(jnp.int32)
    sent = wind_legendre(rot, dil, tmp, pol, orders, limits, band[None])
    got = lax.all_to_all(sent, ("aa", "ba"), split_axis=0, concat_axis=0, tiled=True)
    edges = lax.dynamic_slice_in_dim(limits, band, 2, 0)
    lat = edges[0] + slot
    count = jnp.where(lat < edges[1], jnp.sum(jnp.where(jnp.arange(96) == lat, counts, 0)), 0)
    count = count.astype(jnp.int32)[None]
    tables = make_table(count, wave_row(orders))
    pieces = make_grid(count, got, tables)
    rows = lax.all_to_all(pieces, "ba", split_axis=0, concat_axis=0, tiled=True)
    rows = rows.reshape(BAND_MAX, 2, 3, PIECES, PIECE).astype(F32)
    outs = jnp.transpose(rows, (2, 3, 1, 0, 4)).reshape(3, LEVELS, BAND_MAX, PIECE)
    return outs[0], outs[1], outs[2]


def solution(mesh):
    return jax.shard_map(
        per_device,
        mesh=mesh,
        in_specs=(
            P("ba", None, "aa"),
            P("ba", None, "aa"),
            P("ba", None, "aa"),
            P(None, "aa"),
            P(),
            P(),
            P(),
        ),
        out_specs=(P(None, "aa", "ba"), P(None, "aa", "ba"), P(None, "aa", "ba")),
        check_vma=False,
    )
```

```python
import functools
import math

import jax
import jax.numpy as jnp
from jax import lax
from jax.experimental import pallas as pl
from jax.experimental.pallas import tpu as pltpu
from jax.sharding import PartitionSpec as P

MW = 1280
WIDTH = MW + 1
PAIRS = 80
GROUP = 8
STEPS = PAIRS // GROUP
MAIN = GROUP * MW
WIN = 1408
LATH = 48
BAND_MAX = 16
PIECES = 16
PIECE = 384
LEVELS = 32
KM = 64
KR = PAIRS - KM
KALL = 2 * PAIRS
F32 = jnp.float32
BF16 = jnp.bfloat16
NT = (((1,), (1,)), ((), ()))


def wind_legendre_kernel(
    orders,
    limits,
    where_am_i,
    rot,
    rot_x,
    dil,
    dil_x,
    tmp,
    tmp_x,
    pol,
    pol_x,
    out,
    fields,
    last,
    coef_a,
    coef_b,
    coef_c,
    masks,
    north,
    south,
    tiles,
):
    step = pl.program_id(0)
    me = where_am_i[0]
    live = 102480 - (step + 1) * MAIN

    def edge(ref, lv):
        lane2 = lax.broadcasted_iota(jnp.int32, (2, 128), 1)
        return jnp.where(lane2 < live, ref[lv].astype(F32), 0.0).astype(BF16)

    for src, (ref, ref_x) in enumerate(((rot, rot_x), (dil, dil_x), (tmp, tmp_x), (tmp, tmp_x))):
        for lv in range(2):
            row = src * 4 + lv * 2
            fields[row : row + 2, 0:MAIN] = ref[lv]
            fields[row : row + 2, MAIN : MAIN + 128] = edge(ref_x, lv)
    last[:, 0:MW] = pol[:, MAIN - MW : MAIN]
    lane48 = lax.broadcasted_iota(jnp.int32, (LATH, 128), 1)
    last[:, MW:WIN] = jnp.where(lane48 < live, pol_x[...].astype(F32), 0.0).astype(BF16)

    lane = lax.broadcasted_iota(jnp.int32, (GROUP, WIN), 1)
    sub = lax.broadcasted_iota(jnp.int32, (GROUP, WIN), 0)
    low = [orders[me, 2 * (step * GROUP + s)] for s in range(GROUP)]
    sub1 = lax.broadcasted_iota(jnp.int32, (GROUP, 128), 0)
    lower1 = jnp.zeros((GROUP, 128), jnp.int32)
    for s in range(GROUP):
        lower1 = jnp.where(sub1 == s, low[s], lower1)
    lower = jnp.concatenate([lower1] * (WIN // 128), axis=1)
    pos = lane - sub - step * GROUP
    valid = (pos >= 0) & (pos < WIDTH)
    first = pos < MW - lower
    wave_i = jnp.where(first, lower, MW - 1 - lower)
    deg_i = jnp.where(first, lower + pos, pos - 1)
    even = ((deg_i - wave_i) & 1) == 0
    masks[0] = jnp.where(valid & first & even, 1.0, 0.0)
    masks[1] = jnp.where(valid & first & ~even, 1.0, 0.0)
    masks[2] = jnp.where(valid & ~first & even, 1.0, 0.0)
    masks[3] = jnp.where(valid & ~first & ~even, 1.0, 0.0)
    wave = wave_i.astype(F32)
    usable = valid & (deg_i > 0)
    deg = jnp.where(usable, deg_i, 1).astype(F32)
    square = deg * deg
    eps_over_n = jnp.sqrt(
        jnp.maximum((deg - wave) * (deg + wave), 0.0) / ((4.0 * square - 1.0) * square)
    )
    eps_over_n = jnp.where(usable, eps_over_n, 0.0)
    coef_a[...] = jnp.where(deg > 1.5, eps_over_n, 0.0)
    coef_b[...] = pltpu.roll(eps_over_n, WIN - 1, 1)
    coef_c[...] = jnp.where(usable, wave / (square + deg), 0.0)

    early = step < KM // GROUP
    base = jnp.where(early, step * GROUP, 2 * KM + (step - KM // GROUP) * GROUP)
    seg_off = jnp.where(early, KM, KR)

    row8 = lax.broadcasted_iota(jnp.int32, (8, WIN), 0)
    row_even = (row8 & 1) == 0
    top_half = row8 < 4
    sign = jnp.where(row_even == top_half, 1.0, -1.0)

    def spread(ref, s):
        return ref[pl.ds(s, 8, stride=0), :]

    for s in range(GROUP):
        lo = s * MW
        both = fields[:, lo : lo + WIN].astype(F32)
        x, heat = both[0:8], both[8:16]
        other = jnp.where(row_even, pltpu.roll(x, 3, 0), pltpu.roll(x, 5, 0))
        wind = (
            spread(coef_b, s) * pltpu.roll(x, WIN - 1, 1)
            - spread(coef_a, s) * pltpu.roll(x, 1, 1)
            + spread(coef_c, s) * (other * sign)
        )
        m = [spread(masks.at[g], s) for g in range(4)]
        rows = [wind * m[g] for g in range(4)]
        rows.append(heat * jnp.where(top_half, m[0], m[1]))
        rows.append(heat * jnp.where(top_half, m[2], m[3]))
        data = jnp.concatenate(rows, axis=0).astype(BF16)
        poly = last[...] if s == GROUP - 1 else pol[:, lo : lo + WIN]
        res = lax.dot_general(data, poly, NT, preferred_element_type=F32)
        for seg in range(2):
            at = base + s + seg * seg_off
            plus = res[seg * 16 : seg * 16 + 8]
            minus = res[seg * 16 + 8 : seg * 16 + 16]
            north[pl.ds(at, 8, stride=KALL), :] = plus + minus
            south[pl.ds(at, 8, stride=KALL), :] = plus - minus
            pair = res[32 + seg * 8 : 40 + seg * 8]
            flip = pltpu.roll(pair, 4, 0)
            north[pl.ds(8 * KALL + at, 4, stride=KALL), :] = (pair + flip)[0:4]
            south[pl.ds(8 * KALL + at, 4, stride=KALL), :] = (pair - flip)[0:4]

    @pl.when(step == STEPS - 1)
    def _():
        dest = lax.broadcasted_iota(jnp.int32, (128, LATH), 0)
        column = lax.broadcasted_iota(jnp.int32, (128, LATH), 1)
        lat = dest % BAND_MAX
        for band in range(8):
            lat = lat + jnp.where(dest // BAND_MAX == band, limits[band], 0)
        pick_n = (lat == column).astype(F32).astype(BF16)
        pick_s = (2 * LATH - 1 - lat == column).astype(F32).astype(BF16)

        def rows_of(ref, part, lv, fld, start, size):
            row = fld * 4 + lv * 2 + part
            val = ref[row * KALL + start : row * KALL + start + size, :]
            return (-val if fld == 1 else val).astype(BF16)

        def select(rows_n, rows_s, row):
            val = lax.dot_general(pick_n, rows_n, NT, preferred_element_type=F32)
            val = val + lax.dot_general(pick_s, rows_s, NT, preferred_element_type=F32)
            for block in range(16):
                tiles[pl.ds(row + 128 * block, 8, stride=16), :] = val[8 * block : 8 * block + 8]

        for part in range(2):
            for lv in range(2):
                for fld in range(3):
                    select(
                        rows_of(north, part, lv, fld, 0, 2 * KM),
                        rows_of(south, part, lv, fld, 0, 2 * KM),
                        part * 6 + lv * 3 + fld,
                    )
        for fld in range(3):
            both = []
            for ref in (north, south):
                both.append(
                    jnp.concatenate(
                        [rows_of(ref, q // 2, q % 2, fld, 2 * KM, 2 * KR) for q in range(4)],
                        axis=0,
                    )
                )
            select(both[0], both[1], 12 + fld)
        for block in range(16):
            tiles[pl.ds(15 + 128 * block, 8, stride=16), :] = jnp.zeros((8, 128), F32)
        for block in range(16):
            part = tiles[128 * block : 128 * block + 128, :]
            out[8 * block : 8 * block + 8] = part.reshape(8, 16, 128).astype(BF16)


def wind_legendre(rot, dil, tmp, pol, orders, limits, me):
    def smem(shape):
        return pl.BlockSpec(shape, lambda i: (0,) * len(shape), memory_space=pltpu.SMEM)

    main = pl.BlockSpec((2, 2, MAIN), lambda i: (0, 0, i))
    tail = pl.BlockSpec((2, 2, 128), lambda i: (0, 0, (i + 1) * (MAIN // 128)))
    rot, dil, tmp, pol, orders, limits = (
        pltpu.with_memory_space_constraint(v, pltpu.HBM) for v in (rot, dil, tmp, pol, orders, limits)
    )
    return pl.pallas_call(
        wind_legendre_kernel,
        grid=(STEPS,),
        in_specs=[
            smem((8, 160)),
            smem((9,)),
            smem((1,)),
            main,
            tail,
            main,
            tail,
            main,
            tail,
            pl.BlockSpec((LATH, MAIN), lambda i: (0, i)),
            pl.BlockSpec((LATH, 128), lambda i: (0, (i + 1) * (MAIN // 128))),
        ],
        out_specs=pl.BlockSpec((128, 16, 128), lambda i: (0, 0, 0)),
        out_shape=jax.ShapeDtypeStruct((128, 16, 128), BF16),
        scratch_shapes=[
            pltpu.VMEM((16, MAIN + 128), BF16),
            pltpu.VMEM((LATH, WIN), BF16),
            pltpu.VMEM((GROUP, WIN), F32),
            pltpu.VMEM((GROUP, WIN), F32),
            pltpu.VMEM((GROUP, WIN), F32),
            pltpu.VMEM((4, GROUP, WIN), F32),
            pltpu.VMEM((12 * KALL, LATH), F32),
            pltpu.VMEM((12 * KALL, LATH), F32),
            pltpu.VMEM((2048, 128), F32),
        ],
        compiler_params=pltpu.CompilerParams(vmem_limit_bytes=40 * 1024 * 1024),
        name="wind_legendre",
    )(orders, limits, me, rot, rot, dil, dil, tmp, tmp, pol, pol)


def cos_sin_turns(turns):
    z = turns * (math.pi / 2.0)
    y = z * z
    sin = z * (1.0 + y * (-1 / 6 + y * (1 / 120 + y * (-1 / 5040 + y * (1 / 362880)))))
    cos = 1.0 + y * (-1 / 2 + y * (1 / 24 + y * (-1 / 720 + y * (1 / 40320 + y * (-1 / 3628800)))))
    s2 = 2.0 * sin * cos
    c2 = 1.0 - 2.0 * sin * sin
    return 1.0 - 2.0 * s2 * s2, 2.0 * s2 * c2


def fraction_of_turn(product, count, inverse):
    r = product - jnp.floor(product * inverse + 0.5) * count
    return r * inverse


def table_kernel(count, wave, table, twist_c, twist_s, weight):
    k = count[0].astype(F32)
    k_lane = jnp.maximum(jnp.full((8, 128), k, F32), 1.0)
    inverse = 1.0 / k_lane
    k1, inv1 = k_lane[0:1, 0:1], inverse[0:1, 0:1]
    m_row = wave[...].astype(F32)
    for q in range(2):
        piece = (lax.broadcasted_iota(jnp.int32, (8, MW), 0) + 8 * q).astype(F32)
        cos, sin = cos_sin_turns(fraction_of_turn(piece * m_row, k1, inv1))
        for row in range(8):
            twist_c[8 * q + row] = cos[row : row + 1]
            twist_s[8 * q + row] = sin[row : row + 1]
    top = jnp.full((8, MW), (count[0] - 1) // 2, jnp.int32)
    m8 = jnp.broadcast_to(wave[...], (8, MW))
    w = jnp.where(m8 == 0, 1.0, 2.0)
    weight[...] = jnp.where(m8 <= top, w, 0.0)
    for q in range(MW // 128):
        chunk = jnp.broadcast_to(m_row[:, 128 * q : 128 * q + 128], (128, 128))
        column = jnp.transpose(chunk, (1, 0))
        for c in range(PIECE // 128):
            x = ((lax.broadcasted_iota(jnp.int32, (128, 128), 1) + 128 * c) * PIECES).astype(F32)
            cos, sin = cos_sin_turns(fraction_of_turn(x * column, k1, inv1))
            table[128 * q : 128 * q + 128, 128 * c : 128 * c + 128] = cos.astype(BF16)
            table[MW + 128 * q : MW + 128 * q + 128, 128 * c : 128 * c + 128] = (-sin).astype(BF16)


def make_table(count, wave):
    return pl.pallas_call(
        table_kernel,
        in_specs=[pl.BlockSpec(memory_space=pltpu.SMEM), pl.BlockSpec(memory_space=pltpu.VMEM)],
        out_specs=[pl.BlockSpec(memory_space=pltpu.VMEM)] * 4,
        out_shape=[
            jax.ShapeDtypeStruct((2 * MW, PIECE), BF16),
            jax.ShapeDtypeStruct((PIECES, 1, MW), F32),
            jax.ShapeDtypeStruct((PIECES, 1, MW), F32),
            jax.ShapeDtypeStruct((8, MW), F32),
        ],
        compiler_params=pltpu.CompilerParams(vmem_limit_bytes=32 * 1024 * 1024),
        cost_estimate=pl.CostEstimate(flops=50_000_000, transcendentals=0, bytes_accessed=4_000_000),
        name="trig_table",
    )(count, wave)


PSTEP = 4


def grid_kernel(count, data, table, twist_c, twist_s, weight, out, f_re, f_im, twisted):
    step = pl.program_id(0)

    @pl.when(step == 0)
    def _():
        row = lax.broadcasted_iota(jnp.int32, (192, 256), 0)
        col = lax.broadcasted_iota(jnp.int32, (192, 256), 1)
        pick_main = (col == (row % 16) * 16 + row // 16).astype(F32).astype(BF16)
        pick_rest = (col == (row % 16) * 16 + 12 + (row // 16) % 3).astype(F32).astype(BF16)
        lane = lax.broadcasted_iota(jnp.int32, (48, 128), 1) // 32
        rest = [[jnp.zeros((48, 128), F32) for _ in range(2)] for _ in range(4)]
        for a in range(8):
            x = data[16 * a : 16 * a + 16].reshape(256, 128)
            lanes = slice(128 * a, 128 * a + 128)
            w = weight[0:1, lanes]
            main = jnp.dot(pick_main, x, preferred_element_type=F32)
            f_re[:, lanes] = main[0:96] * w
            f_im[:, lanes] = main[96:192] * w
            more = jnp.dot(pick_rest, x, preferred_element_type=F32)
            for q in range(4):
                piece = more[48 * q : 48 * q + 48]
                shift = (32 * (a % 4) - 32 * q) % 128
                if shift:
                    piece = pltpu.roll(piece, shift, 1)
                rest[q][a // 4] = jnp.where(lane == a % 4, piece, rest[q][a // 4])
        for half in range(2):
            lanes = slice(1024 + 128 * half, 1152 + 128 * half)
            w = weight[0:1, lanes]
            f_re[0:48, lanes] = rest[0][half] * w
            f_re[48:96, lanes] = rest[1][half] * w
            f_im[0:48, lanes] = rest[2][half] * w
            f_im[48:96, lanes] = rest[3][half] * w

    for u in range(PSTEP):
        piece = step * PSTEP + u
        for chunk in range(MW // 128):
            lanes = slice(128 * chunk, 128 * chunk + 128)
            cos = twist_c[piece, :, lanes]
            sin = twist_s[piece, :, lanes]
            re, im = f_re[:, lanes], f_im[:, lanes]
            twisted[96 * u : 96 * u + 96, lanes] = (re * cos - im * sin).astype(BF16)
            twisted[96 * u : 96 * u + 96, MW + 128 * chunk : MW + 128 * chunk + 128] = (
                re * sin + im * cos
            ).astype(BF16)
    res = jnp.dot(twisted[...], table[...], preferred_element_type=F32)
    lon = lax.broadcasted_iota(jnp.int32, (96, PIECE), 1) * PIECES + step * PSTEP
    for u in range(PSTEP):
        keep = lon + u < count[0]
        out[u] = jnp.where(keep, res[96 * u : 96 * u + 96], 0.0).astype(BF16)


def make_grid(count, data, tables):
    def whole(shape):
        return pl.BlockSpec(shape, lambda i: (0,) * len(shape))

    return pl.pallas_call(
        grid_kernel,
        grid=(PIECES // PSTEP,),
        in_specs=[
            pl.BlockSpec((1,), lambda i: (0,), memory_space=pltpu.SMEM),
            whole((128, 16, 128)),
            whole((2 * MW, PIECE)),
            whole((PIECES, 1, MW)),
            whole((PIECES, 1, MW)),
            whole((8, MW)),
        ],
        out_specs=pl.BlockSpec((PSTEP, 96, PIECE), lambda i: (i, 0, 0)),
        out_shape=jax.ShapeDtypeStruct((PIECES, 96, PIECE), BF16),
        scratch_shapes=[
            pltpu.VMEM((96, MW), F32),
            pltpu.VMEM((96, MW), F32),
            pltpu.VMEM((96 * PSTEP, 2 * MW), BF16),
        ],
        compiler_params=pltpu.CompilerParams(vmem_limit_bytes=48 * 1024 * 1024),
        name="grid_product",
    )(count, data, *tables)


def unpack_kernel(rows, out_u, out_v, out_t, wide):
    step = pl.program_id(0)

    @pl.when(step == 0)
    def _():
        for slot in range(BAND_MAX):
            for c in range(PIECE // 128):
                lanes = slice(128 * c, 128 * c + 128)
                wide[c, 96 * slot : 96 * slot + 96, :] = rows[slot, :, lanes].astype(F32)

    for lv in range(2):
        for fld, out in enumerate((out_u, out_v, out_t)):
            for q in range(4):
                row = lv * 48 + fld * 16 + q + step * 4
                for c in range(PIECE // 128):
                    lanes = slice(128 * c, 128 * c + 128)
                    out[2 * q + lv, :, lanes] = wide[c, pl.ds(row, BAND_MAX, stride=96), :]


def unpack(rows):
    leaf = jax.ShapeDtypeStruct((LEVELS, BAND_MAX, PIECE), F32)
    return pl.pallas_call(
        unpack_kernel,
        grid=(4,),
        in_specs=[pl.BlockSpec((BAND_MAX, 96, PIECE), lambda i: (0, 0, 0))],
        out_specs=[pl.BlockSpec((8, BAND_MAX, PIECE), lambda i: (i, 0, 0))] * 3,
        out_shape=[leaf] * 3,
        scratch_shapes=[pltpu.VMEM((PIECE // 128, BAND_MAX * 96, 128), F32)],
        compiler_params=pltpu.CompilerParams(vmem_limit_bytes=24 * 1024 * 1024),
        name="unpack",
    )(rows)


def wave_row(orders):
    lower = orders[:, 0::2]
    both = jnp.stack([lower, MW - 1 - lower], axis=1)
    return jnp.concatenate([both[:, :, :KM].reshape(1, -1), both[:, :, KM:].reshape(1, -1)], axis=1)


def per_device(rot, dil, tmp, pol, orders, counts, limits):
    band = lax.axis_index("aa").astype(jnp.int32)
    slot = lax.axis_index("ba").astype(jnp.int32)
    sent = wind_legendre(rot, dil, tmp, pol, orders, limits, band[None])
    got = lax.all_to_all(sent, ("aa", "ba"), split_axis=0, concat_axis=0, tiled=True)
    edges = lax.dynamic_slice_in_dim(limits, band, 2, 0)
    lat = edges[0] + slot
    count = jnp.where(lat < edges[1], jnp.sum(jnp.where(jnp.arange(96) == lat, counts, 0)), 0)
    count = count.astype(jnp.int32)[None]
    tables = make_table(count, wave_row(orders))
    pieces = make_grid(count, got, tables)
    rows = lax.all_to_all(pieces, "ba", split_axis=0, concat_axis=0, tiled=True)
    return tuple(unpack(rows))


def solution(mesh):
    return jax.shard_map(
        per_device,
        mesh=mesh,
        in_specs=(
            P("ba", None, "aa"),
            P("ba", None, "aa"),
            P("ba", None, "aa"),
            P(None, "aa"),
            P(),
            P(),
            P(),
        ),
        out_specs=(P(None, "aa", "ba"), P(None, "aa", "ba"), P(None, "aa", "ba")),
        check_vma=False,
    )
```

```python
import functools
import math

import jax
import jax.numpy as jnp
from jax import lax
from jax.experimental import pallas as pl
from jax.experimental.pallas import tpu as pltpu
from jax.sharding import PartitionSpec as P

MW = 1280
WIDTH = MW + 1
PAIRS = 80
GROUP = 8
STEPS = PAIRS // GROUP
MAIN = GROUP * MW
WIN = 1408
LATH = 48
BAND_MAX = 16
PIECES = 16
PIECE = 384
LEVELS = 32
KM = 64
KR = PAIRS - KM
KALL = 2 * PAIRS + 1
AHEAD = 2 * MAIN + 128
F32 = jnp.float32
BF16 = jnp.bfloat16
NT = (((1,), (1,)), ((), ()))


def wind_legendre_kernel(
    orders,
    limits,
    where_am_i,
    rot,
    dil,
    tmp,
    pol,
    rot_x,
    dil_x,
    tmp_x,
    pol_x,
    out,
    poly,
    fields,
    coef_a,
    coef_b,
    coef_c,
    masks,
    north,
    south,
    tiles,
    sem_f,
    sem_p,
):
    me = where_am_i[0]
    end = STEPS * MAIN

    def field_copies(half):
        lanes = pl.ds(0, AHEAD) if half == 0 else pl.ds(AHEAD, end - AHEAD)
        for src, ref in enumerate((rot, dil, tmp, tmp)):
            for lv in range(2):
                rows = pl.ds(4 * src + 2 * lv, 2)
                yield pltpu.make_async_copy(
                    ref.at[lv, :, lanes], fields.at[rows, lanes], sem_f.at[half, 2 * src + lv]
                )

    def poly_copy(g, start, size):
        lanes = pl.ds(start, size)
        return pltpu.make_async_copy(pol.at[:, lanes], poly.at[:, lanes], sem_p.at[g])

    def middle(g):
        return poly_copy(g, pl.multiple_of(g * MAIN + 128, 128), MAIN)

    first_poly = poly_copy(0, 0, MAIN + 128)
    last_poly = poly_copy(STEPS - 1, (STEPS - 1) * MAIN + 128, MAIN - 128)
    for copy in field_copies(0):
        copy.start()
    first_poly.start()
    middle(1).start()
    for copy in field_copies(1):
        copy.start()
    for g in range(2, STEPS - 1):
        middle(g).start()
    last_poly.start()

    lane2 = lax.broadcasted_iota(jnp.int32, (2, 128), 1)
    for src, ref in enumerate((rot_x, dil_x, tmp_x, tmp_x)):
        for lv in range(2):
            edge = jnp.where(lane2 < PAIRS, ref[lv].astype(F32), 0.0).astype(BF16)
            fields[4 * src + 2 * lv : 4 * src + 2 * lv + 2, end : end + 128] = edge
    lane48 = lax.broadcasted_iota(jnp.int32, (LATH, 128), 1)
    poly[:, end : end + 128] = jnp.where(lane48 < PAIRS, pol_x[...].astype(F32), 0.0).astype(BF16)

    for copy in field_copies(0):
        copy.wait()
    first_poly.wait()

    def group(step, carry):
        @pl.when((step > 0) & (step < STEPS - 1))
        def _():
            middle(step).wait()

        @pl.when(step == STEPS - 1)
        def _():
            last_poly.wait()

        @pl.when(step == 2)
        def _():
            for copy in field_copies(1):
                copy.wait()

        one_group(step, me, orders, poly, fields, coef_a, coef_b, coef_c, masks, north, south)
        return carry

    lax.fori_loop(0, STEPS, group, 0)
    pack_tiles(limits, out, north, south, tiles)


def one_group(step, me, orders, poly, fields, coef_a, coef_b, coef_c, masks, north, south):
    origin = pl.multiple_of(step * MAIN, 128)

    lane = lax.broadcasted_iota(jnp.int32, (GROUP, WIN), 1)
    sub = lax.broadcasted_iota(jnp.int32, (GROUP, WIN), 0)
    low = [orders[me, 2 * (step * GROUP + s)] for s in range(GROUP)]
    sub1 = lax.broadcasted_iota(jnp.int32, (GROUP, 128), 0)
    lower1 = jnp.zeros((GROUP, 128), jnp.int32)
    for s in range(GROUP):
        lower1 = jnp.where(sub1 == s, low[s], lower1)
    lower = jnp.concatenate([lower1] * (WIN // 128), axis=1)
    pos = lane - sub - step * GROUP
    valid = (pos >= 0) & (pos < WIDTH)
    first = pos < MW - lower
    wave_i = jnp.where(first, lower, MW - 1 - lower)
    deg_i = jnp.where(first, lower + pos, pos - 1)
    masks[0] = jnp.where(valid & first, 1.0, 0.0)
    masks[1] = jnp.where(valid & ~first, 1.0, 0.0)
    wave = wave_i.astype(F32)
    usable = valid & (deg_i > 0)
    deg = jnp.where(usable, deg_i, 1).astype(F32)
    square = deg * deg
    eps_over_n = jnp.sqrt(
        jnp.maximum((deg - wave) * (deg + wave), 0.0) / ((4.0 * square - 1.0) * square)
    )
    eps_over_n = jnp.where(usable, eps_over_n, 0.0)
    coef_a[...] = jnp.where(deg > 1.5, eps_over_n, 0.0)
    coef_b[...] = pltpu.roll(eps_over_n, WIN - 1, 1)
    coef_c[...] = jnp.where(usable, wave / (square + deg), 0.0)

    early = step < KM // GROUP
    base = jnp.where(early, step * GROUP, 2 * KM + (step - KM // GROUP) * GROUP)
    seg_off = jnp.where(early, KM, KR)

    def wide(tile):
        return jnp.concatenate([tile] * (WIN // 128), axis=1)

    row8 = lax.broadcasted_iota(jnp.int32, (8, 128), 0)
    row_even = wide((row8 & 1) == 0)
    sign = wide(jnp.where(((row8 & 1) == 0) == (row8 < 4), 1.0, -1.0))
    row16 = lax.broadcasted_iota(jnp.int32, (16, 128), 0)
    lane16 = lax.broadcasted_iota(jnp.int32, (16, 128), 1)
    alternate = jnp.where((lane16 & 1) == 0, 1.0, -1.0)
    flip_wind = wide(alternate.astype(BF16))
    flip_heat = wide(jnp.where(row16 % 8 < 4, 1.0, alternate).astype(BF16))

    def spread(ref, s):
        return ref[pl.ds(s, 8, stride=0), :]

    results = []
    for s in range(GROUP):
        window = pl.ds(pl.multiple_of(origin + s * MW, 128), WIN)
        both = fields[:, window].astype(F32)
        x, heat = both[0:8], both[8:16]
        other = jnp.where(row_even, pltpu.roll(x, 3, 0), pltpu.roll(x, 5, 0))
        wind = (
            spread(coef_b, s) * pltpu.roll(x, WIN - 1, 1)
            - spread(coef_a, s) * pltpu.roll(x, 1, 1)
            + spread(coef_c, s) * (other * sign)
        )
        m0, m1 = spread(masks.at[0], s), spread(masks.at[1], s)
        winds = jnp.concatenate([wind * m0, wind * m1], axis=0).astype(BF16)
        heats = jnp.concatenate([heat * m0, heat * m1], axis=0).astype(BF16)
        data = jnp.concatenate([winds, winds * flip_wind, heats * flip_heat], axis=0)
        results.append(lax.dot_general(data, poly[:, window], NT, preferred_element_type=F32))
    for s, res in enumerate(results):
        pair = step * GROUP + s
        odd = (pair & 1, (pair + low[s]) & 1)
        for seg in range(2):
            at = base + s + seg * seg_off
            factor = (1 - 2 * odd[seg]).astype(F32)
            north[pl.ds(at, 8, stride=KALL), :] = res[seg * 8 : seg * 8 + 8]
            south[pl.ds(at, 8, stride=KALL), :] = res[16 + seg * 8 : 24 + seg * 8] * factor
            heat = res[32 + seg * 8 : 40 + seg * 8]
            north[pl.ds(8 * KALL + at, 4, stride=KALL), :] = heat[0:4]
            south[pl.ds(8 * KALL + at, 4, stride=KALL), :] = heat[4:8] * factor


def pack_tiles(limits, out, north, south, tiles):
    dest = lax.broadcasted_iota(jnp.int32, (128, LATH), 0)
    column = lax.broadcasted_iota(jnp.int32, (128, LATH), 1)
    lat = dest % BAND_MAX
    for band in range(8):
        lat = lat + jnp.where(dest // BAND_MAX == band, limits[band], 0)
    pick_n = (lat == column).astype(F32).astype(BF16)
    pick_s = (2 * LATH - 1 - lat == column).astype(F32).astype(BF16)

    def rows_of(ref, part, lv, fld, start, size):
        row = fld * 4 + lv * 2 + part
        val = ref[row * KALL + start : row * KALL + start + size, :]
        return (-val if fld == 1 else val).astype(BF16)

    def select(rows_n, rows_s, row):
        val = lax.dot_general(pick_n, rows_n, NT, preferred_element_type=F32)
        val = val + lax.dot_general(pick_s, rows_s, NT, preferred_element_type=F32)
        for block in range(16):
            tiles[pl.ds(row + 128 * block, 8, stride=16), :] = val[8 * block : 8 * block + 8]

    for part in range(2):
        for lv in range(2):
            for fld in range(3):
                select(
                    rows_of(north, part, lv, fld, 0, 2 * KM),
                    rows_of(south, part, lv, fld, 0, 2 * KM),
                    part * 6 + lv * 3 + fld,
                )
    for fld in range(3):
        both = []
        for ref in (north, south):
            both.append(
                jnp.concatenate(
                    [rows_of(ref, q // 2, q % 2, fld, 2 * KM, 2 * KR) for q in range(4)],
                    axis=0,
                )
            )
        select(both[0], both[1], 12 + fld)
    for block in range(16):
        tiles[pl.ds(15 + 128 * block, 8, stride=16), :] = jnp.zeros((8, 128), F32)
    for block in range(16):
        part = tiles[128 * block : 128 * block + 128, :]
        out[8 * block : 8 * block + 8] = part.reshape(8, 16, 128).astype(BF16)


def wind_legendre(rot, dil, tmp, pol, orders, limits, me):
    rot, dil, tmp, pol, orders, limits = (
        pltpu.with_memory_space_constraint(v, pltpu.HBM) for v in (rot, dil, tmp, pol, orders, limits)
    )
    smem = pl.BlockSpec(memory_space=pltpu.SMEM)
    hbm = pl.BlockSpec(memory_space=pltpu.HBM)
    tail = pl.BlockSpec((2, 2, 128), lambda i: (0, 0, PAIRS * MW // 128))
    return pl.pallas_call(
        wind_legendre_kernel,
        grid=(1,),
        in_specs=[
            smem,
            smem,
            smem,
            hbm,
            hbm,
            hbm,
            hbm,
            tail,
            tail,
            tail,
            pl.BlockSpec((LATH, 128), lambda i: (0, PAIRS * MW // 128)),
        ],
        out_specs=pl.BlockSpec((128, 16, 128), lambda i: (0, 0, 0)),
        out_shape=jax.ShapeDtypeStruct((128, 16, 128), BF16),
        scratch_shapes=[
            pltpu.VMEM((LATH, STEPS * MAIN + 128), BF16),
            pltpu.VMEM((16, STEPS * MAIN + 128), BF16),
            pltpu.VMEM((GROUP, WIN), F32),
            pltpu.VMEM((GROUP, WIN), F32),
            pltpu.VMEM((GROUP, WIN), F32),
            pltpu.VMEM((2, GROUP, WIN), F32),
            pltpu.VMEM((12 * KALL, LATH), F32),
            pltpu.VMEM((12 * KALL, LATH), F32),
            pltpu.VMEM((2048, 128), F32),
            pltpu.SemaphoreType.DMA((2, 8)),
            pltpu.SemaphoreType.DMA((STEPS,)),
        ],
        compiler_params=pltpu.CompilerParams(vmem_limit_bytes=40 * 1024 * 1024),
        name="wind_legendre",
    )(orders, limits, me, rot, dil, tmp, pol, rot, dil, tmp, pol)


def cos_sin_turns(turns):
    z = turns * (math.pi / 2.0)
    y = z * z
    sin = z * (1.0 + y * (-1 / 6 + y * (1 / 120 + y * (-1 / 5040 + y * (1 / 362880)))))
    cos = 1.0 + y * (-1 / 2 + y * (1 / 24 + y * (-1 / 720 + y * (1 / 40320 + y * (-1 / 3628800)))))
    s2 = 2.0 * sin * cos
    c2 = 1.0 - 2.0 * sin * sin
    return 1.0 - 2.0 * s2 * s2, 2.0 * s2 * c2


def fraction_of_turn(product, count, inverse):
    r = product - jnp.floor(product * inverse + 0.5) * count
    return r * inverse


def table_kernel(count, wave, table, twist_c, twist_s, weight):
    k = count[0].astype(F32)
    k_lane = jnp.maximum(jnp.full((8, 128), k, F32), 1.0)
    inverse = 1.0 / k_lane
    k1, inv1 = k_lane[0:1, 0:1], inverse[0:1, 0:1]
    m_row = wave[...].astype(F32)
    for q in range(2):
        piece = (lax.broadcasted_iota(jnp.int32, (8, MW), 0) + 8 * q).astype(F32)
        cos, sin = cos_sin_turns(fraction_of_turn(piece * m_row, k1, inv1))
        for row in range(8):
            twist_c[8 * q + row] = cos[row : row + 1]
            twist_s[8 * q + row] = sin[row : row + 1]
    top = jnp.full((8, MW), (count[0] - 1) // 2, jnp.int32)
    m8 = jnp.broadcast_to(wave[...], (8, MW))
    w = jnp.where(m8 == 0, 1.0, 2.0)
    weight[...] = jnp.where(m8 <= top, w, 0.0)
    for q in range(MW // 128):
        chunk = jnp.broadcast_to(m_row[:, 128 * q : 128 * q + 128], (128, 128))
        column = jnp.transpose(chunk, (1, 0))
        for c in range(PIECE // 128):
            x = ((lax.broadcasted_iota(jnp.int32, (128, 128), 1) + 128 * c) * PIECES).astype(F32)
            cos, sin = cos_sin_turns(fraction_of_turn(x * column, k1, inv1))
            table[128 * q : 128 * q + 128, 128 * c : 128 * c + 128] = cos.astype(BF16)
            table[MW + 128 * q : MW + 128 * q + 128, 128 * c : 128 * c + 128] = (-sin).astype(BF16)


def make_table(count, wave):
    return pl.pallas_call(
        table_kernel,
        in_specs=[pl.BlockSpec(memory_space=pltpu.SMEM), pl.BlockSpec(memory_space=pltpu.VMEM)],
        out_specs=[pl.BlockSpec(memory_space=pltpu.VMEM)] * 4,
        out_shape=[
            jax.ShapeDtypeStruct((2 * MW, PIECE), BF16),
            jax.ShapeDtypeStruct((PIECES, 1, MW), F32),
            jax.ShapeDtypeStruct((PIECES, 1, MW), F32),
            jax.ShapeDtypeStruct((8, MW), F32),
        ],
        compiler_params=pltpu.CompilerParams(vmem_limit_bytes=32 * 1024 * 1024),
        cost_estimate=pl.CostEstimate(flops=50_000_000, transcendentals=0, bytes_accessed=4_000_000),
        name="trig_table",
    )(count, wave)


PSTEP = 4


def grid_kernel(count, data, table, twist_c, twist_s, weight, out, f_re, f_im, twisted):
    step = pl.program_id(0)

    @pl.when(step == 0)
    def _():
        row = lax.broadcasted_iota(jnp.int32, (192, 256), 0)
        col = lax.broadcasted_iota(jnp.int32, (192, 256), 1)
        pick_main = (col == (row % 16) * 16 + row // 16).astype(F32).astype(BF16)
        pick_rest = (col == (row % 16) * 16 + 12 + (row // 16) % 3).astype(F32).astype(BF16)
        lane = lax.broadcasted_iota(jnp.int32, (48, 128), 1) // 32
        rest = [[jnp.zeros((48, 128), F32) for _ in range(2)] for _ in range(4)]
        for a in range(8):
            x = data[16 * a : 16 * a + 16].reshape(256, 128)
            lanes = slice(128 * a, 128 * a + 128)
            w = weight[0:1, lanes]
            main = jnp.dot(pick_main, x, preferred_element_type=F32)
            f_re[:, lanes] = main[0:96] * w
            f_im[:, lanes] = main[96:192] * w
            more = jnp.dot(pick_rest, x, preferred_element_type=F32)
            for q in range(4):
                piece = more[48 * q : 48 * q + 48]
                shift = (32 * (a % 4) - 32 * q) % 128
                if shift:
                    piece = pltpu.roll(piece, shift, 1)
                rest[q][a // 4] = jnp.where(lane == a % 4, piece, rest[q][a // 4])
        for half in range(2):
            lanes = slice(1024 + 128 * half, 1152 + 128 * half)
            w = weight[0:1, lanes]
            f_re[0:48, lanes] = rest[0][half] * w
            f_re[48:96, lanes] = rest[1][half] * w
            f_im[0:48, lanes] = rest[2][half] * w
            f_im[48:96, lanes] = rest[3][half] * w

    for u in range(PSTEP):
        piece = step * PSTEP + u
        for chunk in range(MW // 128):
            lanes = slice(128 * chunk, 128 * chunk + 128)
            cos = twist_c[piece, :, lanes]
            sin = twist_s[piece, :, lanes]
            re, im = f_re[:, lanes], f_im[:, lanes]
            twisted[96 * u : 96 * u + 96, lanes] = (re * cos - im * sin).astype(BF16)
            twisted[96 * u : 96 * u + 96, MW + 128 * chunk : MW + 128 * chunk + 128] = (
                re * sin + im * cos
            ).astype(BF16)
    res = jnp.dot(twisted[...], table[...], preferred_element_type=F32)
    lon = lax.broadcasted_iota(jnp.int32, (96, PIECE), 1) * PIECES + step * PSTEP
    for u in range(PSTEP):
        keep = lon + u < count[0]
        out[u] = jnp.where(keep, res[96 * u : 96 * u + 96], 0.0).astype(BF16)


def make_grid(count, data, tables):
    def whole(shape):
        return pl.BlockSpec(shape, lambda i: (0,) * len(shape))

    return pl.pallas_call(
        grid_kernel,
        grid=(PIECES // PSTEP,),
        in_specs=[
            pl.BlockSpec((1,), lambda i: (0,), memory_space=pltpu.SMEM),
            whole((128, 16, 128)),
            whole((2 * MW, PIECE)),
            whole((PIECES, 1, MW)),
            whole((PIECES, 1, MW)),
            whole((8, MW)),
        ],
        out_specs=pl.BlockSpec((PSTEP, 96, PIECE), lambda i: (i, 0, 0)),
        out_shape=jax.ShapeDtypeStruct((PIECES, 96, PIECE), BF16),
        scratch_shapes=[
            pltpu.VMEM((96, MW), F32),
            pltpu.VMEM((96, MW), F32),
            pltpu.VMEM((96 * PSTEP, 2 * MW), BF16),
        ],
        compiler_params=pltpu.CompilerParams(vmem_limit_bytes=48 * 1024 * 1024),
        name="grid_product",
    )(count, data, *tables)


def unpack_kernel(rows, out_u, out_v, out_t, wide):
    for slot in range(BAND_MAX):
        wide[97 * slot : 97 * slot + 96, :] = rows[slot].astype(F32)
    for lv in range(2):
        for fld, out in enumerate((out_u, out_v, out_t)):
            for src in range(16):
                row = lv * 48 + fld * 16 + src
                out[2 * src + lv] = wide[pl.ds(row, BAND_MAX, stride=97), :]


def unpack(rows):
    leaf = jax.ShapeDtypeStruct((LEVELS, BAND_MAX, PIECE), F32)
    return pl.pallas_call(
        unpack_kernel,
        grid=(PIECE // 128,),
        in_specs=[pl.BlockSpec((BAND_MAX, 96, 128), lambda i: (0, 0, i))],
        out_specs=[pl.BlockSpec((LEVELS, BAND_MAX, 128), lambda i: (0, 0, i))] * 3,
        out_shape=[leaf] * 3,
        scratch_shapes=[pltpu.VMEM((BAND_MAX * 97, 128), F32)],
        compiler_params=pltpu.CompilerParams(vmem_limit_bytes=24 * 1024 * 1024),
        name="unpack",
    )(rows)


def wave_row(orders):
    lower = orders[:, 0::2]
    both = jnp.stack([lower, MW - 1 - lower], axis=1)
    return jnp.concatenate([both[:, :, :KM].reshape(1, -1), both[:, :, KM:].reshape(1, -1)], axis=1)


def per_device(rot, dil, tmp, pol, orders, counts, limits):
    band = lax.axis_index("aa").astype(jnp.int32)
    slot = lax.axis_index("ba").astype(jnp.int32)
    sent = wind_legendre(rot, dil, tmp, pol, orders, limits, band[None])
    got = lax.all_to_all(sent, ("aa", "ba"), split_axis=0, concat_axis=0, tiled=True)
    edges = lax.dynamic_slice_in_dim(limits, band, 2, 0)
    lat = edges[0] + slot
    count = jnp.where(lat < edges[1], jnp.sum(jnp.where(jnp.arange(96) == lat, counts, 0)), 0)
    count = count.astype(jnp.int32)[None]
    tables = make_table(count, wave_row(orders))
    pieces = make_grid(count, got, tables)
    rows = lax.all_to_all(pieces, "ba", split_axis=0, concat_axis=0, tiled=True)
    return tuple(unpack(rows))


def solution(mesh):
    return jax.shard_map(
        per_device,
        mesh=mesh,
        in_specs=(
            P("ba", None, "aa"),
            P("ba", None, "aa"),
            P("ba", None, "aa"),
            P(None, "aa"),
            P(),
            P(),
            P(),
        ),
        out_specs=(P(None, "aa", "ba"), P(None, "aa", "ba"), P(None, "aa", "ba")),
        check_vma=False,
    )
```

```python
import functools
import math

import jax
import jax.numpy as jnp
from jax import lax
from jax.experimental import pallas as pl
from jax.experimental.pallas import tpu as pltpu
from jax.sharding import PartitionSpec as P

MW = 1280
WIDTH = MW + 1
PAIRS = 80
GROUP = 16
STEPS = PAIRS // GROUP
MAIN = GROUP * MW
WIN = 1408
LATH = 48
BAND_MAX = 16
PIECES = 16
PIECE = 384
LEVELS = 32
KM = 64
KR = PAIRS - KM
KALL = 2 * PAIRS + 1
BLOCK = 16
BLOCKS = PAIRS // BLOCK
PART = BLOCK * MW
AHEAD = 2
F32 = jnp.float32
BF16 = jnp.bfloat16
NT = (((1,), (1,)), ((), ()))


def wind_legendre_kernel(
    orders,
    limits,
    where_am_i,
    rot,
    dil,
    tmp,
    pol,
    rot_x,
    dil_x,
    tmp_x,
    pol_x,
    out,
    poly,
    fields,
    coef_a,
    coef_b,
    coef_c,
    masks,
    north,
    south,
    tiles,
    sem_f,
    sem_p,
):
    me = where_am_i[0]
    end = STEPS * MAIN

    def span(g, start, size):
        lanes = pl.ds(start, size)
        for src, ref in enumerate((rot, dil, tmp, tmp)):
            for lv in range(2):
                rows = pl.ds(4 * src + 2 * lv, 2)
                yield pltpu.make_async_copy(
                    ref.at[lv, :, lanes], fields.at[rows, lanes], sem_f.at[2 * src + lv, g]
                )
        yield pltpu.make_async_copy(pol.at[:, lanes], poly.at[:, lanes], sem_p.at[g])

    def copies(g):
        return span(g, pl.multiple_of(g * PART + 128, 128), PART)

    def first_copies():
        return span(0, 0, PART + 128)

    def last_copies():
        return span(BLOCKS - 1, (BLOCKS - 1) * PART + 128, PART - 128)

    for copy in first_copies():
        copy.start()
    for g in range(1, AHEAD):
        for copy in copies(g):
            copy.start()

    lane2 = lax.broadcasted_iota(jnp.int32, (2, 128), 1)
    for src, ref in enumerate((rot_x, dil_x, tmp_x, tmp_x)):
        for lv in range(2):
            edge = jnp.where(lane2 < PAIRS, ref[lv].astype(F32), 0.0).astype(BF16)
            fields[4 * src + 2 * lv : 4 * src + 2 * lv + 2, end : end + 128] = edge
    lane48 = lax.broadcasted_iota(jnp.int32, (LATH, 128), 1)
    poly[:, end : end + 128] = jnp.where(lane48 < PAIRS, pol_x[...].astype(F32), 0.0).astype(BF16)

    for copy in first_copies():
        copy.wait()

    def turn(block):
        @pl.when((block > 0) & (block < BLOCKS - 1))
        def _():
            for copy in copies(block):
                copy.wait()

        @pl.when(block == BLOCKS - 1)
        def _():
            for copy in last_copies():
                copy.wait()

        @pl.when(block + AHEAD < BLOCKS - 1)
        def _():
            for copy in copies(block + AHEAD):
                copy.start()

        @pl.when(block + AHEAD == BLOCKS - 1)
        def _():
            for copy in last_copies():
                copy.start()

    def group(step, carry):
        one_group(step, turn, me, orders, poly, fields, coef_a, coef_b, coef_c, masks, north, south)
        return carry

    lax.fori_loop(0, STEPS, group, 0)
    pack_tiles(limits, out, north, south, tiles)


def one_group(step, turn, me, orders, poly, fields, coef_a, coef_b, coef_c, masks, north, south):
    origin = pl.multiple_of(step * MAIN, 128)

    lane = lax.broadcasted_iota(jnp.int32, (GROUP, WIN), 1)
    sub = lax.broadcasted_iota(jnp.int32, (GROUP, WIN), 0)
    low = [orders[me, 2 * (step * GROUP + s)] for s in range(GROUP)]
    sub1 = lax.broadcasted_iota(jnp.int32, (GROUP, 128), 0)
    lower1 = jnp.zeros((GROUP, 128), jnp.int32)
    for s in range(GROUP):
        lower1 = jnp.where(sub1 == s, low[s], lower1)
    lower = jnp.concatenate([lower1] * (WIN // 128), axis=1)
    pos = lane - sub - step * GROUP
    valid = (pos >= 0) & (pos < WIDTH)
    first = pos < MW - lower
    wave_i = jnp.where(first, lower, MW - 1 - lower)
    deg_i = jnp.where(first, lower + pos, pos - 1)
    masks[0] = jnp.where(valid & first, 1.0, 0.0)
    masks[1] = jnp.where(valid & ~first, 1.0, 0.0)
    wave = wave_i.astype(F32)
    usable = valid & (deg_i > 0)
    deg = jnp.where(usable, deg_i, 1).astype(F32)
    square = deg * deg
    eps_over_n = jnp.sqrt(
        jnp.maximum((deg - wave) * (deg + wave), 0.0) / ((4.0 * square - 1.0) * square)
    )
    eps_over_n = jnp.where(usable, eps_over_n, 0.0)
    coef_a[...] = jnp.where(deg > 1.5, eps_over_n, 0.0)
    coef_b[...] = pltpu.roll(eps_over_n, WIN - 1, 1)
    coef_c[...] = jnp.where(usable, wave / (square + deg), 0.0)

    early = step < KM // GROUP
    base = jnp.where(early, step * GROUP, 2 * KM + (step - KM // GROUP) * GROUP)
    seg_off = jnp.where(early, KM, KR)

    def wide(tile):
        return jnp.concatenate([tile] * (WIN // 128), axis=1)

    row8 = lax.broadcasted_iota(jnp.int32, (8, 128), 0)
    row_even = wide((row8 & 1) == 0)
    sign = wide(jnp.where(((row8 & 1) == 0) == (row8 < 4), 1.0, -1.0))
    row16 = lax.broadcasted_iota(jnp.int32, (16, 128), 0)
    lane16 = lax.broadcasted_iota(jnp.int32, (16, 128), 1)
    alternate = jnp.where((lane16 & 1) == 0, 1.0, -1.0)
    flip_wind = wide(alternate.astype(BF16))
    flip_heat = wide(jnp.where(row16 % 8 < 4, 1.0, alternate).astype(BF16))

    def spread(ref, s):
        return ref[pl.ds(s, 8, stride=0), :]

    results = []
    for s in range(GROUP):
        if s % BLOCK == 0:
            turn(step * (GROUP // BLOCK) + s // BLOCK)
        window = pl.ds(pl.multiple_of(origin + s * MW, 128), WIN)
        both = fields[:, window].astype(F32)
        x, heat = both[0:8], both[8:16]
        other = jnp.where(row_even, pltpu.roll(x, 3, 0), pltpu.roll(x, 5, 0))
        wind = (
            spread(coef_b, s) * pltpu.roll(x, WIN - 1, 1)
            - spread(coef_a, s) * pltpu.roll(x, 1, 1)
            + spread(coef_c, s) * (other * sign)
        )
        m0, m1 = spread(masks.at[0], s), spread(masks.at[1], s)
        winds = jnp.concatenate([wind * m0, wind * m1], axis=0).astype(BF16)
        heats = jnp.concatenate([heat * m0, heat * m1], axis=0).astype(BF16)
        data = jnp.concatenate([winds, winds * flip_wind, heats * flip_heat], axis=0)
        results.append(lax.dot_general(data, poly[:, window], NT, preferred_element_type=F32))
    for s, res in enumerate(results):
        pair = step * GROUP + s
        odd = (pair & 1, (pair + low[s]) & 1)
        for seg in range(2):
            at = base + s + seg * seg_off
            factor = (1 - 2 * odd[seg]).astype(F32)
            north[pl.ds(at, 8, stride=KALL), :] = res[seg * 8 : seg * 8 + 8]
            south[pl.ds(at, 8, stride=KALL), :] = res[16 + seg * 8 : 24 + seg * 8] * factor
            heat = res[32 + seg * 8 : 40 + seg * 8]
            north[pl.ds(8 * KALL + at, 4, stride=KALL), :] = heat[0:4]
            south[pl.ds(8 * KALL + at, 4, stride=KALL), :] = heat[4:8] * factor


def pack_tiles(limits, out, north, south, tiles):
    dest = lax.broadcasted_iota(jnp.int32, (128, LATH), 0)
    column = lax.broadcasted_iota(jnp.int32, (128, LATH), 1)
    lat = dest % BAND_MAX
    for band in range(8):
        lat = lat + jnp.where(dest // BAND_MAX == band, limits[band], 0)
    pick_n = (lat == column).astype(F32).astype(BF16)
    pick_s = (2 * LATH - 1 - lat == column).astype(F32).astype(BF16)

    def rows_of(ref, part, lv, fld, start, size):
        row = fld * 4 + lv * 2 + part
        val = ref[row * KALL + start : row * KALL + start + size, :]
        return (-val if fld == 1 else val).astype(BF16)

    def select(rows_n, rows_s, row):
        val = lax.dot_general(pick_n, rows_n, NT, preferred_element_type=F32)
        val = val + lax.dot_general(pick_s, rows_s, NT, preferred_element_type=F32)
        for block in range(16):
            tiles[pl.ds(row + 128 * block, 8, stride=16), :] = val[8 * block : 8 * block + 8]

    for part in range(2):
        for lv in range(2):
            for fld in range(3):
                select(
                    rows_of(north, part, lv, fld, 0, 2 * KM),
                    rows_of(south, part, lv, fld, 0, 2 * KM),
                    part * 6 + lv * 3 + fld,
                )
    for fld in range(3):
        both = []
        for ref in (north, south):
            both.append(
                jnp.concatenate(
                    [rows_of(ref, q // 2, q % 2, fld, 2 * KM, 2 * KR) for q in range(4)],
                    axis=0,
                )
            )
        select(both[0], both[1], 12 + fld)
    for block in range(16):
        tiles[pl.ds(15 + 128 * block, 8, stride=16), :] = jnp.zeros((8, 128), F32)
    for block in range(16):
        part = tiles[128 * block : 128 * block + 128, :]
        out[8 * block : 8 * block + 8] = part.reshape(8, 16, 128).astype(BF16)


def wind_legendre(rot, dil, tmp, pol, orders, limits, me):
    rot, dil, tmp, pol, orders, limits = (
        pltpu.with_memory_space_constraint(v, pltpu.HBM) for v in (rot, dil, tmp, pol, orders, limits)
    )
    smem = pl.BlockSpec(memory_space=pltpu.SMEM)
    hbm = pl.BlockSpec(memory_space=pltpu.HBM)
    tail = pl.BlockSpec((2, 2, 128), lambda i: (0, 0, PAIRS * MW // 128))
    return pl.pallas_call(
        wind_legendre_kernel,
        grid=(1,),
        in_specs=[
            smem,
            smem,
            smem,
            hbm,
            hbm,
            hbm,
            hbm,
            tail,
            tail,
            tail,
            pl.BlockSpec((LATH, 128), lambda i: (0, PAIRS * MW // 128)),
        ],
        out_specs=pl.BlockSpec((128, 16, 128), lambda i: (0, 0, 0)),
        out_shape=jax.ShapeDtypeStruct((128, 16, 128), BF16),
        scratch_shapes=[
            pltpu.VMEM((LATH, STEPS * MAIN + 128), BF16),
            pltpu.VMEM((16, STEPS * MAIN + 128), BF16),
            pltpu.VMEM((GROUP, WIN), F32),
            pltpu.VMEM((GROUP, WIN), F32),
            pltpu.VMEM((GROUP, WIN), F32),
            pltpu.VMEM((2, GROUP, WIN), F32),
            pltpu.VMEM((12 * KALL, LATH), F32),
            pltpu.VMEM((12 * KALL, LATH), F32),
            pltpu.VMEM((2048, 128), F32),
            pltpu.SemaphoreType.DMA((8, BLOCKS)),
            pltpu.SemaphoreType.DMA((BLOCKS,)),
        ],
        compiler_params=pltpu.CompilerParams(vmem_limit_bytes=40 * 1024 * 1024),
        name="wind_legendre",
    )(orders, limits, me, rot, dil, tmp, pol, rot, dil, tmp, pol)


def cos_sin_turns(turns):
    z = turns * (math.pi / 2.0)
    y = z * z
    sin = z * (1.0 + y * (-1 / 6 + y * (1 / 120 + y * (-1 / 5040 + y * (1 / 362880)))))
    cos = 1.0 + y * (-1 / 2 + y * (1 / 24 + y * (-1 / 720 + y * (1 / 40320 + y * (-1 / 3628800)))))
    s2 = 2.0 * sin * cos
    c2 = 1.0 - 2.0 * sin * sin
    return 1.0 - 2.0 * s2 * s2, 2.0 * s2 * c2


def fraction_of_turn(product, count, inverse):
    r = product - jnp.floor(product * inverse + 0.5) * count
    return r * inverse


def table_kernel(count, wave, table, twist_c, twist_s, weight):
    k = count[0].astype(F32)
    k_lane = jnp.maximum(jnp.full((8, 128), k, F32), 1.0)
    inverse = 1.0 / k_lane
    k1, inv1 = k_lane[0:1, 0:1], inverse[0:1, 0:1]
    m_row = wave[...].astype(F32)
    for q in range(2):
        piece = (lax.broadcasted_iota(jnp.int32, (8, MW), 0) + 8 * q).astype(F32)
        cos, sin = cos_sin_turns(fraction_of_turn(piece * m_row, k1, inv1))
        for row in range(8):
            twist_c[8 * q + row] = cos[row : row + 1]
            twist_s[8 * q + row] = sin[row : row + 1]
    top = jnp.full((8, MW), (count[0] - 1) // 2, jnp.int32)
    m8 = jnp.broadcast_to(wave[...], (8, MW))
    w = jnp.where(m8 == 0, 1.0, 2.0)
    weight[...] = jnp.where(m8 <= top, w, 0.0)
    for q in range(MW // 128):
        chunk = jnp.broadcast_to(m_row[:, 128 * q : 128 * q + 128], (128, 128))
        column = jnp.transpose(chunk, (1, 0))
        for c in range(PIECE // 128):
            x = ((lax.broadcasted_iota(jnp.int32, (128, 128), 1) + 128 * c) * PIECES).astype(F32)
            cos, sin = cos_sin_turns(fraction_of_turn(x * column, k1, inv1))
            table[128 * q : 128 * q + 128, 128 * c : 128 * c + 128] = cos.astype(BF16)
            table[MW + 128 * q : MW + 128 * q + 128, 128 * c : 128 * c + 128] = (-sin).astype(BF16)


def make_table(count, wave):
    return pl.pallas_call(
        table_kernel,
        in_specs=[pl.BlockSpec(memory_space=pltpu.SMEM), pl.BlockSpec(memory_space=pltpu.VMEM)],
        out_specs=[pl.BlockSpec(memory_space=pltpu.VMEM)] * 4,
        out_shape=[
            jax.ShapeDtypeStruct((2 * MW, PIECE), BF16),
            jax.ShapeDtypeStruct((PIECES, 1, MW), F32),
            jax.ShapeDtypeStruct((PIECES, 1, MW), F32),
            jax.ShapeDtypeStruct((8, MW), F32),
        ],
        compiler_params=pltpu.CompilerParams(vmem_limit_bytes=32 * 1024 * 1024),
        cost_estimate=pl.CostEstimate(flops=50_000_000, transcendentals=0, bytes_accessed=4_000_000),
        name="trig_table",
    )(count, wave)


PSTEP = 4


def grid_kernel(count, data, table, twist_c, twist_s, weight, out, f_re, f_im, twisted):
    step = pl.program_id(0)

    @pl.when(step == 0)
    def _():
        row = lax.broadcasted_iota(jnp.int32, (192, 256), 0)
        col = lax.broadcasted_iota(jnp.int32, (192, 256), 1)
        pick_main = (col == (row % 16) * 16 + row // 16).astype(F32).astype(BF16)
        pick_rest = (col == (row % 16) * 16 + 12 + (row // 16) % 3).astype(F32).astype(BF16)
        lane = lax.broadcasted_iota(jnp.int32, (48, 128), 1) // 32
        rest = [[jnp.zeros((48, 128), F32) for _ in range(2)] for _ in range(4)]
        for a in range(8):
            x = data[16 * a : 16 * a + 16].reshape(256, 128)
            lanes = slice(128 * a, 128 * a + 128)
            w = weight[0:1, lanes]
            main = jnp.dot(pick_main, x, preferred_element_type=F32)
            f_re[:, lanes] = main[0:96] * w
            f_im[:, lanes] = main[96:192] * w
            more = jnp.dot(pick_rest, x, preferred_element_type=F32)
            for q in range(4):
                piece = more[48 * q : 48 * q + 48]
                shift = (32 * (a % 4) - 32 * q) % 128
                if shift:
                    piece = pltpu.roll(piece, shift, 1)
                rest[q][a // 4] = jnp.where(lane == a % 4, piece, rest[q][a // 4])
        for half in range(2):
            lanes = slice(1024 + 128 * half, 1152 + 128 * half)
            w = weight[0:1, lanes]
            f_re[0:48, lanes] = rest[0][half] * w
            f_re[48:96, lanes] = rest[1][half] * w
            f_im[0:48, lanes] = rest[2][half] * w
            f_im[48:96, lanes] = rest[3][half] * w

    for u in range(PSTEP):
        piece = step * PSTEP + u
        for chunk in range(MW // 128):
            lanes = slice(128 * chunk, 128 * chunk + 128)
            cos = twist_c[piece, :, lanes]
            sin = twist_s[piece, :, lanes]
            re, im = f_re[:, lanes], f_im[:, lanes]
            twisted[96 * u : 96 * u + 96, lanes] = (re * cos - im * sin).astype(BF16)
            twisted[96 * u : 96 * u + 96, MW + 128 * chunk : MW + 128 * chunk + 128] = (
                re * sin + im * cos
            ).astype(BF16)
    res = jnp.dot(twisted[...], table[...], preferred_element_type=F32)
    lon = lax.broadcasted_iota(jnp.int32, (96, PIECE), 1) * PIECES + step * PSTEP
    for u in range(PSTEP):
        keep = lon + u < count[0]
        out[u] = jnp.where(keep, res[96 * u : 96 * u + 96], 0.0).astype(BF16)


def make_grid(count, data, tables):
    def whole(shape):
        return pl.BlockSpec(shape, lambda i: (0,) * len(shape))

    return pl.pallas_call(
        grid_kernel,
        grid=(PIECES // PSTEP,),
        in_specs=[
            pl.BlockSpec((1,), lambda i: (0,), memory_space=pltpu.SMEM),
            whole((128, 16, 128)),
            whole((2 * MW, PIECE)),
            whole((PIECES, 1, MW)),
            whole((PIECES, 1, MW)),
            whole((8, MW)),
        ],
        out_specs=pl.BlockSpec((PSTEP, 96, PIECE), lambda i: (i, 0, 0)),
        out_shape=jax.ShapeDtypeStruct((PIECES, 96, PIECE), BF16),
        scratch_shapes=[
            pltpu.VMEM((96, MW), F32),
            pltpu.VMEM((96, MW), F32),
            pltpu.VMEM((96 * PSTEP, 2 * MW), BF16),
        ],
        compiler_params=pltpu.CompilerParams(vmem_limit_bytes=48 * 1024 * 1024),
        name="grid_product",
    )(count, data, *tables)


def unpack_kernel(rows, out_u, out_v, out_t, wide):
    for slot in range(BAND_MAX):
        wide[97 * slot : 97 * slot + 96, :] = rows[slot].astype(F32)
    for lv in range(2):
        for fld, out in enumerate((out_u, out_v, out_t)):
            for src in range(16):
                row = lv * 48 + fld * 16 + src
                out[2 * src + lv] = wide[pl.ds(row, BAND_MAX, stride=97), :]


def unpack(rows):
    leaf = jax.ShapeDtypeStruct((LEVELS, BAND_MAX, PIECE), F32)
    return pl.pallas_call(
        unpack_kernel,
        grid=(PIECE // 128,),
        in_specs=[pl.BlockSpec((BAND_MAX, 96, 128), lambda i: (0, 0, i))],
        out_specs=[pl.BlockSpec((LEVELS, BAND_MAX, 128), lambda i: (0, 0, i))] * 3,
        out_shape=[leaf] * 3,
        scratch_shapes=[pltpu.VMEM((BAND_MAX * 97, 128), F32)],
        compiler_params=pltpu.CompilerParams(vmem_limit_bytes=24 * 1024 * 1024),
        name="unpack",
    )(rows)


def wave_row(orders):
    lower = orders[:, 0::2]
    both = jnp.stack([lower, MW - 1 - lower], axis=1)
    return jnp.concatenate([both[:, :, :KM].reshape(1, -1), both[:, :, KM:].reshape(1, -1)], axis=1)


def per_device(rot, dil, tmp, pol, orders, counts, limits):
    band = lax.axis_index("aa").astype(jnp.int32)
    slot = lax.axis_index("ba").astype(jnp.int32)
    sent = wind_legendre(rot, dil, tmp, pol, orders, limits, band[None])
    got = lax.all_to_all(sent, ("aa", "ba"), split_axis=0, concat_axis=0, tiled=True)
    edges = lax.dynamic_slice_in_dim(limits, band, 2, 0)
    lat = edges[0] + slot
    count = jnp.where(lat < edges[1], jnp.sum(jnp.where(jnp.arange(96) == lat, counts, 0)), 0)
    count = count.astype(jnp.int32)[None]
    tables = make_table(count, wave_row(orders))
    pieces = make_grid(count, got, tables)
    rows = lax.all_to_all(pieces, "ba", split_axis=0, concat_axis=0, tiled=True)
    return tuple(unpack(rows))


def solution(mesh):
    return jax.shard_map(
        per_device,
        mesh=mesh,
        in_specs=(
            P("ba", None, "aa"),
            P("ba", None, "aa"),
            P("ba", None, "aa"),
            P(None, "aa"),
            P(),
            P(),
            P(),
        ),
        out_specs=(P(None, "aa", "ba"), P(None, "aa", "ba"), P(None, "aa", "ba")),
        check_vma=False,
    )
```

```python
import functools
import math

import jax
import jax.numpy as jnp
from jax import lax
from jax.experimental import pallas as pl
from jax.experimental.pallas import tpu as pltpu
from jax.sharding import PartitionSpec as P

MW = 1280
WIDTH = MW + 1
PAIRS = 80
GROUP = 16
STEPS = PAIRS // GROUP
MAIN = GROUP * MW
WIN = 1408
LATH = 48
BAND_MAX = 16
PIECES = 16
PIECE = 384
LEVELS = 32
KM = 64
KR = PAIRS - KM
KALL = 2 * PAIRS + 1
AHEAD = 2
F32 = jnp.float32
BF16 = jnp.bfloat16
NT = (((1,), (1,)), ((), ()))


def wind_legendre_kernel(
    orders,
    limits,
    where_am_i,
    rot,
    dil,
    tmp,
    pol,
    rot_x,
    dil_x,
    tmp_x,
    pol_x,
    out,
    poly,
    fields,
    coef_a,
    coef_b,
    coef_c,
    masks,
    north,
    south,
    tiles,
    sem_f,
    sem_p,
):
    me = where_am_i[0]
    end = STEPS * MAIN

    def span(g, start, size):
        lanes = pl.ds(start, size)
        for src, ref in enumerate((rot, dil, tmp, tmp)):
            for lv in range(2):
                rows = pl.ds(4 * src + 2 * lv, 2)
                yield pltpu.make_async_copy(
                    ref.at[lv, :, lanes], fields.at[rows, lanes], sem_f.at[2 * src + lv, g]
                )
        yield pltpu.make_async_copy(pol.at[:, lanes], poly.at[:, lanes], sem_p.at[g])

    def copies(g):
        return span(g, pl.multiple_of(g * MAIN + 128, 128), MAIN)

    def first_copies():
        return span(0, 0, MAIN + 128)

    def last_copies():
        return span(STEPS - 1, (STEPS - 1) * MAIN + 128, MAIN - 128)

    for copy in first_copies():
        copy.start()
    for g in range(1, AHEAD):
        for copy in copies(g):
            copy.start()

    lane2 = lax.broadcasted_iota(jnp.int32, (2, 128), 1)
    for src, ref in enumerate((rot_x, dil_x, tmp_x, tmp_x)):
        for lv in range(2):
            edge = jnp.where(lane2 < PAIRS, ref[lv].astype(F32), 0.0).astype(BF16)
            fields[4 * src + 2 * lv : 4 * src + 2 * lv + 2, end : end + 128] = edge
    lane48 = lax.broadcasted_iota(jnp.int32, (LATH, 128), 1)
    poly[:, end : end + 128] = jnp.where(lane48 < PAIRS, pol_x[...].astype(F32), 0.0).astype(BF16)

    for copy in first_copies():
        copy.wait()

    def turn(block):
        @pl.when((block > 0) & (block < STEPS - 1))
        def _():
            for copy in copies(block):
                copy.wait()

        @pl.when(block == STEPS - 1)
        def _():
            for copy in last_copies():
                copy.wait()

        @pl.when(block + AHEAD < STEPS - 1)
        def _():
            for copy in copies(block + AHEAD):
                copy.start()

        @pl.when(block + AHEAD == STEPS - 1)
        def _():
            for copy in last_copies():
                copy.start()

    def group(step, carry):
        one_group(step, turn, me, orders, poly, fields, coef_a, coef_b, coef_c, masks, north, south)
        return carry

    lax.fori_loop(0, STEPS, group, 0)
    pack_tiles(limits, out, north, south, tiles)


def one_group(step, turn, me, orders, poly, fields, coef_a, coef_b, coef_c, masks, north, south):
    turn(step)
    origin = pl.multiple_of(step * MAIN, 128)

    lane = lax.broadcasted_iota(jnp.int32, (GROUP, WIN), 1)
    sub = lax.broadcasted_iota(jnp.int32, (GROUP, WIN), 0)
    low = [orders[me, 2 * (step * GROUP + s)] for s in range(GROUP)]
    sub1 = lax.broadcasted_iota(jnp.int32, (GROUP, 128), 0)
    lower1 = jnp.zeros((GROUP, 128), jnp.int32)
    for s in range(GROUP):
        lower1 = jnp.where(sub1 == s, low[s], lower1)
    lower = jnp.concatenate([lower1] * (WIN // 128), axis=1)
    pos = lane - sub - step * GROUP
    valid = (pos >= 0) & (pos < WIDTH)
    first = pos < MW - lower
    wave_i = jnp.where(first, lower, MW - 1 - lower)
    deg_i = jnp.where(first, lower + pos, pos - 1)
    masks[0] = jnp.where(valid & first, 1.0, 0.0)
    masks[1] = jnp.where(valid & ~first, 1.0, 0.0)
    wave = wave_i.astype(F32)
    usable = valid & (deg_i > 0)
    deg = jnp.where(usable, deg_i, 1).astype(F32)
    square = deg * deg
    eps_over_n = jnp.sqrt(
        jnp.maximum((deg - wave) * (deg + wave), 0.0) / ((4.0 * square - 1.0) * square)
    )
    eps_over_n = jnp.where(usable, eps_over_n, 0.0)
    coef_a[...] = jnp.where(deg > 1.5, eps_over_n, 0.0)
    coef_b[...] = pltpu.roll(eps_over_n, WIN - 1, 1)
    coef_c[...] = jnp.where(usable, wave / (square + deg), 0.0)

    early = step < KM // GROUP
    base = jnp.where(early, step * GROUP, 2 * KM + (step - KM // GROUP) * GROUP)
    seg_off = jnp.where(early, KM, KR)

    def wide(tile):
        return jnp.concatenate([tile] * (WIN // 128), axis=1)

    row8 = lax.broadcasted_iota(jnp.int32, (8, 128), 0)
    row_even = wide((row8 & 1) == 0)
    sign = wide(jnp.where(((row8 & 1) == 0) == (row8 < 4), 1.0, -1.0))
    row16 = lax.broadcasted_iota(jnp.int32, (16, 128), 0)
    lane16 = lax.broadcasted_iota(jnp.int32, (16, 128), 1)
    alternate = jnp.where((lane16 & 1) == 0, 1.0, -1.0)
    flip_wind = wide(alternate.astype(BF16))
    flip_heat = wide(jnp.where(row16 % 8 < 4, 1.0, alternate).astype(BF16))

    def spread(ref, s):
        return ref[pl.ds(s, 8, stride=0), :]

    results = []
    for s in range(GROUP):
        window = pl.ds(pl.multiple_of(origin + s * MW, 128), WIN)
        both = fields[:, window].astype(F32)
        x, heat = both[0:8], both[8:16]
        other = jnp.where(row_even, pltpu.roll(x, 3, 0), pltpu.roll(x, 5, 0))
        wind = (
            spread(coef_b, s) * pltpu.roll(x, WIN - 1, 1)
            - spread(coef_a, s) * pltpu.roll(x, 1, 1)
            + spread(coef_c, s) * (other * sign)
        )
        m0, m1 = spread(masks.at[0], s), spread(masks.at[1], s)
        winds = jnp.concatenate([wind * m0, wind * m1], axis=0).astype(BF16)
        heats = jnp.concatenate([heat * m0, heat * m1], axis=0).astype(BF16)
        data = jnp.concatenate([winds, winds * flip_wind, heats * flip_heat], axis=0)
        results.append(lax.dot_general(data, poly[:, window], NT, preferred_element_type=F32))
    for s, res in enumerate(results):
        pair = step * GROUP + s
        odd = (pair & 1, (pair + low[s]) & 1)
        for seg in range(2):
            at = base + s + seg * seg_off
            factor = (1 - 2 * odd[seg]).astype(F32)
            north[pl.ds(at, 8, stride=KALL), :] = res[seg * 8 : seg * 8 + 8]
            south[pl.ds(at, 8, stride=KALL), :] = res[16 + seg * 8 : 24 + seg * 8] * factor
            heat = res[32 + seg * 8 : 40 + seg * 8]
            north[pl.ds(8 * KALL + at, 4, stride=KALL), :] = heat[0:4]
            south[pl.ds(8 * KALL + at, 4, stride=KALL), :] = heat[4:8] * factor


def pack_tiles(limits, out, north, south, tiles):
    dest = lax.broadcasted_iota(jnp.int32, (128, LATH), 0)
    column = lax.broadcasted_iota(jnp.int32, (128, LATH), 1)
    lat = dest % BAND_MAX
    for band in range(8):
        lat = lat + jnp.where(dest // BAND_MAX == band, limits[band], 0)
    pick_n = (lat == column).astype(F32).astype(BF16)
    pick_s = (2 * LATH - 1 - lat == column).astype(F32).astype(BF16)

    def rows_of(ref, part, lv, fld, start, size):
        row = fld * 4 + lv * 2 + part
        val = ref[row * KALL + start : row * KALL + start + size, :]
        return (-val if fld == 1 else val).astype(BF16)

    def select(rows_n, rows_s, row):
        val = lax.dot_general(pick_n, rows_n, NT, preferred_element_type=F32)
        val = val + lax.dot_general(pick_s, rows_s, NT, preferred_element_type=F32)
        for block in range(16):
            tiles[pl.ds(row + 128 * block, 8, stride=16), :] = val[8 * block : 8 * block + 8]

    for part in range(2):
        for lv in range(2):
            for fld in range(3):
                select(
                    rows_of(north, part, lv, fld, 0, 2 * KM),
                    rows_of(south, part, lv, fld, 0, 2 * KM),
                    part * 6 + lv * 3 + fld,
                )
    for fld in range(3):
        both = []
        for ref in (north, south):
            both.append(
                jnp.concatenate(
                    [rows_of(ref, q // 2, q % 2, fld, 2 * KM, 2 * KR) for q in range(4)],
                    axis=0,
                )
            )
        select(both[0], both[1], 12 + fld)
    for block in range(16):
        tiles[pl.ds(15 + 128 * block, 8, stride=16), :] = jnp.zeros((8, 128), F32)
    for block in range(16):
        part = tiles[128 * block : 128 * block + 128, :]
        out[8 * block : 8 * block + 8] = part.reshape(8, 16, 128).astype(BF16)


def wind_legendre(rot, dil, tmp, pol, orders, limits, me):
    rot, dil, tmp, pol, orders, limits = (
        pltpu.with_memory_space_constraint(v, pltpu.HBM) for v in (rot, dil, tmp, pol, orders, limits)
    )
    smem = pl.BlockSpec(memory_space=pltpu.SMEM)
    hbm = pl.BlockSpec(memory_space=pltpu.HBM)
    tail = pl.BlockSpec((2, 2, 128), lambda i: (0, 0, PAIRS * MW // 128))
    return pl.pallas_call(
        wind_legendre_kernel,
        grid=(1,),
        in_specs=[
            smem,
            smem,
            smem,
            hbm,
            hbm,
            hbm,
            hbm,
            tail,
            tail,
            tail,
            pl.BlockSpec((LATH, 128), lambda i: (0, PAIRS * MW // 128)),
        ],
        out_specs=pl.BlockSpec((128, 16, 128), lambda i: (0, 0, 0)),
        out_shape=jax.ShapeDtypeStruct((128, 16, 128), BF16),
        scratch_shapes=[
            pltpu.VMEM((LATH, STEPS * MAIN + 128), BF16),
            pltpu.VMEM((16, STEPS * MAIN + 128), BF16),
            pltpu.VMEM((GROUP, WIN), F32),
            pltpu.VMEM((GROUP, WIN), F32),
            pltpu.VMEM((GROUP, WIN), F32),
            pltpu.VMEM((2, GROUP, WIN), F32),
            pltpu.VMEM((12 * KALL, LATH), F32),
            pltpu.VMEM((12 * KALL, LATH), F32),
            pltpu.VMEM((2048, 128), F32),
            pltpu.SemaphoreType.DMA((8, STEPS)),
            pltpu.SemaphoreType.DMA((STEPS,)),
        ],
        compiler_params=pltpu.CompilerParams(vmem_limit_bytes=40 * 1024 * 1024),
        name="wind_legendre",
    )(orders, limits, me, rot, dil, tmp, pol, rot, dil, tmp, pol)


def cos_sin_turns(turns):
    z = turns * (math.pi / 2.0)
    y = z * z
    sin = z * (1.0 + y * (-1 / 6 + y * (1 / 120 + y * (-1 / 5040 + y * (1 / 362880)))))
    cos = 1.0 + y * (-1 / 2 + y * (1 / 24 + y * (-1 / 720 + y * (1 / 40320 + y * (-1 / 3628800)))))
    s2 = 2.0 * sin * cos
    c2 = 1.0 - 2.0 * sin * sin
    return 1.0 - 2.0 * s2 * s2, 2.0 * s2 * c2


def fraction_of_turn(product, count, inverse):
    r = product - jnp.floor(product * inverse + 0.5) * count
    return r * inverse


def table_kernel(count, wave, table, twist_c, twist_s, weight):
    k = count[0].astype(F32)
    k_lane = jnp.maximum(jnp.full((8, 128), k, F32), 1.0)
    inverse = 1.0 / k_lane
    k1, inv1 = k_lane[0:1, 0:1], inverse[0:1, 0:1]
    m_row = wave[...].astype(F32)
    for q in range(2):
        piece = (lax.broadcasted_iota(jnp.int32, (8, MW), 0) + 8 * q).astype(F32)
        cos, sin = cos_sin_turns(fraction_of_turn(piece * m_row, k1, inv1))
        for row in range(8):
            twist_c[8 * q + row] = cos[row : row + 1]
            twist_s[8 * q + row] = sin[row : row + 1]
    top = jnp.full((8, MW), (count[0] - 1) // 2, jnp.int32)
    m8 = jnp.broadcast_to(wave[...], (8, MW))
    w = jnp.where(m8 == 0, 1.0, 2.0)
    weight[...] = jnp.where(m8 <= top, w, 0.0)
    for q in range(MW // 128):
        chunk = jnp.broadcast_to(m_row[:, 128 * q : 128 * q + 128], (128, 128))
        column = jnp.transpose(chunk, (1, 0))
        for c in range(PIECE // 128):
            x = ((lax.broadcasted_iota(jnp.int32, (128, 128), 1) + 128 * c) * PIECES).astype(F32)
            cos, sin = cos_sin_turns(fraction_of_turn(x * column, k1, inv1))
            table[128 * q : 128 * q + 128, 128 * c : 128 * c + 128] = cos.astype(BF16)
            table[MW + 128 * q : MW + 128 * q + 128, 128 * c : 128 * c + 128] = (-sin).astype(BF16)


def make_table(count, wave):
    return pl.pallas_call(
        table_kernel,
        in_specs=[pl.BlockSpec(memory_space=pltpu.SMEM), pl.BlockSpec(memory_space=pltpu.VMEM)],
        out_specs=[pl.BlockSpec(memory_space=pltpu.VMEM)] * 4,
        out_shape=[
            jax.ShapeDtypeStruct((2 * MW, PIECE), BF16),
            jax.ShapeDtypeStruct((PIECES, 1, MW), F32),
            jax.ShapeDtypeStruct((PIECES, 1, MW), F32),
            jax.ShapeDtypeStruct((8, MW), F32),
        ],
        compiler_params=pltpu.CompilerParams(vmem_limit_bytes=32 * 1024 * 1024),
        cost_estimate=pl.CostEstimate(flops=50_000_000, transcendentals=0, bytes_accessed=4_000_000),
        name="trig_table",
    )(count, wave)


PSTEP = 4
SENT = 248


def grid_kernel(count, data, table, twist_c, twist_s, weight, out, f_re, f_im, twisted):
    step = pl.program_id(0)

    @pl.when(step == 0)
    def _():
        row = lax.broadcasted_iota(jnp.int32, (192, 256), 0)
        col = lax.broadcasted_iota(jnp.int32, (192, 256), 1)
        pick_main = (col == (row % 16) * 16 + row // 16).astype(F32).astype(BF16)
        pick_rest = (col == (row % 16) * 16 + 12 + (row // 16) % 3).astype(F32).astype(BF16)
        lane = lax.broadcasted_iota(jnp.int32, (48, 128), 1) // 32
        rest = [[jnp.zeros((48, 128), F32) for _ in range(2)] for _ in range(4)]
        for a in range(8):
            x = data[16 * a : 16 * a + 16].reshape(256, 128)
            lanes = slice(128 * a, 128 * a + 128)
            w = weight[0:1, lanes]
            main = jnp.dot(pick_main, x, preferred_element_type=F32)
            f_re[:, lanes] = main[0:96] * w
            f_im[:, lanes] = main[96:192] * w
            more = jnp.dot(pick_rest, x, preferred_element_type=F32)
            for q in range(4):
                piece = more[48 * q : 48 * q + 48]
                shift = (32 * (a % 4) - 32 * q) % 128
                if shift:
                    piece = pltpu.roll(piece, shift, 1)
                rest[q][a // 4] = jnp.where(lane == a % 4, piece, rest[q][a // 4])
        for half in range(2):
            lanes = slice(1024 + 128 * half, 1152 + 128 * half)
            w = weight[0:1, lanes]
            f_re[0:48, lanes] = rest[0][half] * w
            f_re[48:96, lanes] = rest[1][half] * w
            f_im[0:48, lanes] = rest[2][half] * w
            f_im[48:96, lanes] = rest[3][half] * w

    for u in range(PSTEP):
        piece = step * PSTEP + u
        for chunk in range(MW // 128):
            lanes = slice(128 * chunk, 128 * chunk + 128)
            cos = twist_c[piece, :, lanes]
            sin = twist_s[piece, :, lanes]
            re, im = f_re[:, lanes], f_im[:, lanes]
            twisted[96 * u : 96 * u + 96, lanes] = (re * cos - im * sin).astype(BF16)
            twisted[96 * u : 96 * u + 96, MW + 128 * chunk : MW + 128 * chunk + 128] = (
                re * sin + im * cos
            ).astype(BF16)
    res = jnp.dot(twisted[...], table[...], preferred_element_type=F32)
    lon = lax.broadcasted_iota(jnp.int32, (96, PIECE), 1) * PIECES + step * PSTEP
    left = lax.broadcasted_iota(jnp.int32, (48, 128), 1) < 64
    pick_row = lax.broadcasted_iota(jnp.int32, (8, 128), 0) == 0
    pick_col = lax.broadcasted_iota(jnp.int32, (8, 128), 1) == 64
    pick = (pick_row & pick_col).astype(F32).astype(BF16)
    for u in range(PSTEP):
        keep = lon + u < count[0]
        val = jnp.where(keep, res[96 * u : 96 * u + 96], 0.0)
        out[u, 0:96] = val[:, 0:128].astype(BF16)
        out[u, 96:192] = val[:, 128:256].astype(BF16)
        rest = val[:, 256:384]
        out[u, 192:240] = jnp.where(left, rest[0:48], pltpu.roll(rest[48:96], 64, 1)).astype(BF16)
        rest = jnp.concatenate([rest, jnp.zeros((32, 128), F32)], axis=0).astype(BF16)
        last = lax.dot_general(pick, rest, NT, preferred_element_type=F32)
        out[u, 240:SENT] = last.astype(BF16)


def make_grid(count, data, tables):
    def whole(shape):
        return pl.BlockSpec(shape, lambda i: (0,) * len(shape))

    return pl.pallas_call(
        grid_kernel,
        grid=(PIECES // PSTEP,),
        in_specs=[
            pl.BlockSpec((1,), lambda i: (0,), memory_space=pltpu.SMEM),
            whole((128, 16, 128)),
            whole((2 * MW, PIECE)),
            whole((PIECES, 1, MW)),
            whole((PIECES, 1, MW)),
            whole((8, MW)),
        ],
        out_specs=pl.BlockSpec((PSTEP, SENT, 128), lambda i: (i, 0, 0)),
        out_shape=jax.ShapeDtypeStruct((PIECES, SENT, 128), BF16),
        scratch_shapes=[
            pltpu.VMEM((96, MW), F32),
            pltpu.VMEM((96, MW), F32),
            pltpu.VMEM((96 * PSTEP, 2 * MW), BF16),
        ],
        compiler_params=pltpu.CompilerParams(vmem_limit_bytes=48 * 1024 * 1024),
        name="grid_product",
    )(count, data, *tables)


def unpack_kernel(rows, out_u, out_v, out_t, wide):
    step = pl.program_id(0)
    for part in range(2):

        @pl.when(step == part)
        def _(part=part):
            for slot in range(BAND_MAX):
                chunk = rows[slot, 96 * part : 96 * part + 96]
                wide[97 * slot : 97 * slot + 96, :] = chunk.astype(F32)

    @pl.when(step == 2)
    def _():
        left = lax.broadcasted_iota(jnp.int32, (48, 128), 1) < 64
        pick_row = lax.broadcasted_iota(jnp.int32, (8, 128), 0) == 0
        pick_col = lax.broadcasted_iota(jnp.int32, (8, 128), 1) == 64
        pick = (pick_row & pick_col).astype(F32).astype(BF16)
        for slot in range(BAND_MAX):
            both = rows[slot, 192:240].astype(F32)
            last = lax.dot_general(
                rows[slot, 240:SENT], pick, (((0,), (0,)), ((), ())), preferred_element_type=F32
            )
            for half, val in enumerate((both, pltpu.roll(both, 64, 1))):
                val = jnp.where(left, val, 0.0) + last[48 * half : 48 * half + 48]
                wide[97 * slot + 48 * half : 97 * slot + 48 * half + 48, :] = val

    for lv in range(2):
        for fld, out in enumerate((out_u, out_v, out_t)):
            for src in range(16):
                row = lv * 48 + fld * 16 + src
                out[2 * src + lv] = wide[pl.ds(row, BAND_MAX, stride=97), :]


def unpack(rows):
    leaf = jax.ShapeDtypeStruct((LEVELS, BAND_MAX, PIECE), F32)
    return pl.pallas_call(
        unpack_kernel,
        grid=(PIECE // 128,),
        in_specs=[pl.BlockSpec((BAND_MAX, SENT, 128), lambda i: (0, 0, 0))],
        out_specs=[pl.BlockSpec((LEVELS, BAND_MAX, 128), lambda i: (0, 0, i))] * 3,
        out_shape=[leaf] * 3,
        scratch_shapes=[pltpu.VMEM((BAND_MAX * 97, 128), F32)],
        compiler_params=pltpu.CompilerParams(vmem_limit_bytes=24 * 1024 * 1024),
        name="unpack",
    )(rows)


def wave_row(orders):
    lower = orders[:, 0::2]
    both = jnp.stack([lower, MW - 1 - lower], axis=1)
    return jnp.concatenate([both[:, :, :KM].reshape(1, -1), both[:, :, KM:].reshape(1, -1)], axis=1)


def per_device(rot, dil, tmp, pol, orders, counts, limits):
    band = lax.axis_index("aa").astype(jnp.int32)
    slot = lax.axis_index("ba").astype(jnp.int32)
    sent = wind_legendre(rot, dil, tmp, pol, orders, limits, band[None])
    got = lax.all_to_all(sent, ("aa", "ba"), split_axis=0, concat_axis=0, tiled=True)
    edges = lax.dynamic_slice_in_dim(limits, band, 2, 0)
    lat = edges[0] + slot
    count = jnp.where(lat < edges[1], jnp.sum(jnp.where(jnp.arange(96) == lat, counts, 0)), 0)
    count = count.astype(jnp.int32)[None]
    tables = make_table(count, wave_row(orders))
    pieces = make_grid(count, got, tables)
    rows = lax.all_to_all(pieces, "ba", split_axis=0, concat_axis=0, tiled=True)
    return tuple(unpack(rows))


def solution(mesh):
    return jax.shard_map(
        per_device,
        mesh=mesh,
        in_specs=(
            P("ba", None, "aa"),
            P("ba", None, "aa"),
            P("ba", None, "aa"),
            P(None, "aa"),
            P(),
            P(),
            P(),
        ),
        out_specs=(P(None, "aa", "ba"), P(None, "aa", "ba"), P(None, "aa", "ba")),
        check_vma=False,
    )
```

```python
import functools
import math

import jax
import jax.numpy as jnp
from jax import lax
from jax.experimental import pallas as pl
from jax.experimental.pallas import tpu as pltpu
from jax.sharding import PartitionSpec as P

MW = 1280
WIDTH = MW + 1
PAIRS = 80
GROUP = 16
STEPS = PAIRS // GROUP
MAIN = GROUP * MW
WIN = 1408
LATH = 48
BAND_MAX = 16
PIECES = 16
PIECE = 384
LEVELS = 32
KM = 64
KR = PAIRS - KM
KALL = 2 * PAIRS + 1
AHEAD = 2
F32 = jnp.float32
BF16 = jnp.bfloat16
NT = (((1,), (1,)), ((), ()))


def wind_legendre_kernel(
    orders,
    limits,
    where_am_i,
    rot,
    dil,
    tmp,
    pol,
    rot_x,
    dil_x,
    tmp_x,
    pol_x,
    out,
    poly,
    fields,
    coef_a,
    coef_b,
    coef_c,
    masks,
    north,
    south,
    tiles,
    sem_f,
    sem_p,
):
    me = where_am_i[0]
    end = STEPS * MAIN

    def span(g, start, size):
        lanes = pl.ds(start, size)
        for src, ref in enumerate((rot, dil, tmp, tmp)):
            for lv in range(2):
                rows = pl.ds(4 * src + 2 * lv, 2)
                yield pltpu.make_async_copy(
                    ref.at[lv, :, lanes], fields.at[rows, lanes], sem_f.at[2 * src + lv, g]
                )
        yield pltpu.make_async_copy(pol.at[:, lanes], poly.at[:, lanes], sem_p.at[g])

    def copies(g):
        return span(g, pl.multiple_of(g * MAIN + 128, 128), MAIN)

    def first_copies():
        return span(0, 0, MAIN + 128)

    def last_copies():
        return span(STEPS - 1, (STEPS - 1) * MAIN + 128, MAIN - 128)

    for copy in first_copies():
        copy.start()
    for g in range(1, AHEAD):
        for copy in copies(g):
            copy.start()

    lane2 = lax.broadcasted_iota(jnp.int32, (2, 128), 1)
    for src, ref in enumerate((rot_x, dil_x, tmp_x, tmp_x)):
        for lv in range(2):
            edge = jnp.where(lane2 < PAIRS, ref[lv].astype(F32), 0.0).astype(BF16)
            fields[4 * src + 2 * lv : 4 * src + 2 * lv + 2, end : end + 128] = edge
    lane48 = lax.broadcasted_iota(jnp.int32, (LATH, 128), 1)
    poly[:, end : end + 128] = jnp.where(lane48 < PAIRS, pol_x[...].astype(F32), 0.0).astype(BF16)

    for copy in first_copies():
        copy.wait()

    def turn(block):
        @pl.when((block > 0) & (block < STEPS - 1))
        def _():
            for copy in copies(block):
                copy.wait()

        @pl.when(block == STEPS - 1)
        def _():
            for copy in last_copies():
                copy.wait()

        @pl.when(block + AHEAD < STEPS - 1)
        def _():
            for copy in copies(block + AHEAD):
                copy.start()

        @pl.when(block + AHEAD == STEPS - 1)
        def _():
            for copy in last_copies():
                copy.start()

    def group(step, carry):
        one_group(step, turn, me, orders, poly, fields, coef_a, coef_b, coef_c, masks, north, south)
        return carry

    lax.fori_loop(0, STEPS, group, 0)
    pack_tiles(limits, out, north, south, tiles)


def one_group(step, turn, me, orders, poly, fields, coef_a, coef_b, coef_c, masks, north, south):
    turn(step)
    origin = pl.multiple_of(step * MAIN, 128)

    lane = lax.broadcasted_iota(jnp.int32, (GROUP, WIN), 1)
    sub = lax.broadcasted_iota(jnp.int32, (GROUP, WIN), 0)
    low = [orders[me, 2 * (step * GROUP + s)] for s in range(GROUP)]
    sub1 = lax.broadcasted_iota(jnp.int32, (GROUP, 128), 0)
    lower1 = jnp.zeros((GROUP, 128), jnp.int32)
    for s in range(GROUP):
        lower1 = jnp.where(sub1 == s, low[s], lower1)
    lower = jnp.concatenate([lower1] * (WIN // 128), axis=1)
    pos = lane - sub - step * GROUP
    valid = (pos >= 0) & (pos < WIDTH)
    first = pos < MW - lower
    wave_i = jnp.where(first, lower, MW - 1 - lower)
    deg_i = jnp.where(first, lower + pos, pos - 1)
    masks[0] = jnp.where(valid & first, 1.0, 0.0)
    masks[1] = jnp.where(valid & ~first, 1.0, 0.0)
    wave = wave_i.astype(F32)
    usable = valid & (deg_i > 0)
    deg = jnp.where(usable, deg_i, 1).astype(F32)
    square = deg * deg
    eps_over_n = jnp.sqrt(
        jnp.maximum((deg - wave) * (deg + wave), 0.0) / ((4.0 * square - 1.0) * square)
    )
    eps_over_n = jnp.where(usable, eps_over_n, 0.0)
    coef_a[...] = jnp.where(deg > 1.5, eps_over_n, 0.0)
    coef_b[...] = pltpu.roll(eps_over_n, WIN - 1, 1)
    coef_c[...] = jnp.where(usable, wave / (square + deg), 0.0)

    early = step < KM // GROUP
    base = jnp.where(early, step * GROUP, 2 * KM + (step - KM // GROUP) * GROUP)
    seg_off = jnp.where(early, KM, KR)

    def wide(tile):
        return jnp.concatenate([tile] * (WIN // 128), axis=1)

    row8 = lax.broadcasted_iota(jnp.int32, (8, 128), 0)
    row_even = wide((row8 & 1) == 0)
    sign = wide(jnp.where(((row8 & 1) == 0) == (row8 < 4), 1.0, -1.0))
    row16 = lax.broadcasted_iota(jnp.int32, (16, 128), 0)
    lane16 = lax.broadcasted_iota(jnp.int32, (16, 128), 1)
    alternate = jnp.where((lane16 & 1) == 0, 1.0, -1.0)
    flip_wind = wide(alternate.astype(BF16))
    flip_heat = wide(jnp.where(row16 % 8 < 4, 1.0, alternate).astype(BF16))

    def spread(ref, s):
        return ref[pl.ds(s, 8, stride=0), :]

    results = []
    for s in range(GROUP):
        window = pl.ds(pl.multiple_of(origin + s * MW, 128), WIN)
        both = fields[:, window].astype(F32)
        x, heat = both[0:8], both[8:16]
        other = jnp.where(row_even, pltpu.roll(x, 3, 0), pltpu.roll(x, 5, 0))
        wind = (
            spread(coef_b, s) * pltpu.roll(x, WIN - 1, 1)
            - spread(coef_a, s) * pltpu.roll(x, 1, 1)
            + spread(coef_c, s) * (other * sign)
        )
        m0, m1 = spread(masks.at[0], s), spread(masks.at[1], s)
        winds = jnp.concatenate([wind * m0, wind * m1], axis=0).astype(BF16)
        heats = jnp.concatenate([heat * m0, heat * m1], axis=0).astype(BF16)
        data = jnp.concatenate([winds, winds * flip_wind, heats * flip_heat], axis=0)
        results.append(lax.dot_general(data, poly[:, window], NT, preferred_element_type=F32))
    for s, res in enumerate(results):
        pair = step * GROUP + s
        odd = (pair & 1, (pair + low[s]) & 1)
        for seg in range(2):
            at = base + s + seg * seg_off
            factor = (1 - 2 * odd[seg]).astype(F32)
            north[pl.ds(at, 8, stride=KALL), :] = res[seg * 8 : seg * 8 + 8]
            south[pl.ds(at, 8, stride=KALL), :] = res[16 + seg * 8 : 24 + seg * 8] * factor
            heat = res[32 + seg * 8 : 40 + seg * 8]
            north[pl.ds(8 * KALL + at, 4, stride=KALL), :] = heat[0:4]
            south[pl.ds(8 * KALL + at, 4, stride=KALL), :] = heat[4:8] * factor


def pack_tiles(limits, out, north, south, tiles):
    dest = lax.broadcasted_iota(jnp.int32, (128, LATH), 0)
    column = lax.broadcasted_iota(jnp.int32, (128, LATH), 1)
    lat = dest % BAND_MAX
    for band in range(8):
        lat = lat + jnp.where(dest // BAND_MAX == band, limits[band], 0)
    pick_n = (lat == column).astype(F32).astype(BF16)
    pick_s = (2 * LATH - 1 - lat == column).astype(F32).astype(BF16)

    def rows_of(ref, part, lv, fld, start, size):
        row = fld * 4 + lv * 2 + part
        val = ref[row * KALL + start : row * KALL + start + size, :]
        return (-val if fld == 1 else val).astype(BF16)

    def select(rows_n, rows_s, row):
        val = lax.dot_general(pick_n, rows_n, NT, preferred_element_type=F32)
        val = val + lax.dot_general(pick_s, rows_s, NT, preferred_element_type=F32)
        for block in range(16):
            tiles[pl.ds(row + 128 * block, 8, stride=16), :] = val[8 * block : 8 * block + 8]

    for part in range(2):
        for lv in range(2):
            for fld in range(3):
                select(
                    rows_of(north, part, lv, fld, 0, 2 * KM),
                    rows_of(south, part, lv, fld, 0, 2 * KM),
                    part * 6 + lv * 3 + fld,
                )
    for fld in range(3):
        both = []
        for ref in (north, south):
            both.append(
                jnp.concatenate(
                    [rows_of(ref, q // 2, q % 2, fld, 2 * KM, 2 * KR) for q in range(4)],
                    axis=0,
                )
            )
        select(both[0], both[1], 12 + fld)
    for block in range(16):
        tiles[pl.ds(15 + 128 * block, 8, stride=16), :] = jnp.zeros((8, 128), F32)
    for block in range(16):
        part = tiles[128 * block : 128 * block + 128, :]
        out[8 * block : 8 * block + 8] = part.reshape(8, 16, 128).astype(BF16)


def wind_legendre(rot, dil, tmp, pol, orders, limits, me):
    rot, dil, tmp, pol, orders, limits = (
        pltpu.with_memory_space_constraint(v, pltpu.HBM) for v in (rot, dil, tmp, pol, orders, limits)
    )
    smem = pl.BlockSpec(memory_space=pltpu.SMEM)
    hbm = pl.BlockSpec(memory_space=pltpu.HBM)
    tail = pl.BlockSpec((2, 2, 128), lambda i: (0, 0, PAIRS * MW // 128))
    return pl.pallas_call(
        wind_legendre_kernel,
        grid=(1,),
        in_specs=[
            smem,
            smem,
            smem,
            hbm,
            hbm,
            hbm,
            hbm,
            tail,
            tail,
            tail,
            pl.BlockSpec((LATH, 128), lambda i: (0, PAIRS * MW // 128)),
        ],
        out_specs=pl.BlockSpec((128, 16, 128), lambda i: (0, 0, 0)),
        out_shape=jax.ShapeDtypeStruct((128, 16, 128), BF16),
        scratch_shapes=[
            pltpu.VMEM((LATH, STEPS * MAIN + 128), BF16),
            pltpu.VMEM((16, STEPS * MAIN + 128), BF16),
            pltpu.VMEM((GROUP, WIN), F32),
            pltpu.VMEM((GROUP, WIN), F32),
            pltpu.VMEM((GROUP, WIN), F32),
            pltpu.VMEM((2, GROUP, WIN), F32),
            pltpu.VMEM((12 * KALL, LATH), F32),
            pltpu.VMEM((12 * KALL, LATH), F32),
            pltpu.VMEM((2048, 128), F32),
            pltpu.SemaphoreType.DMA((8, STEPS)),
            pltpu.SemaphoreType.DMA((STEPS,)),
        ],
        compiler_params=pltpu.CompilerParams(vmem_limit_bytes=40 * 1024 * 1024),
        name="wind_legendre",
    )(orders, limits, me, rot, dil, tmp, pol, rot, dil, tmp, pol)


def cos_sin_turns(turns):
    z = turns * (math.pi / 2.0)
    y = z * z
    sin = z * (1.0 + y * (-1 / 6 + y * (1 / 120 + y * (-1 / 5040 + y * (1 / 362880)))))
    cos = 1.0 + y * (-1 / 2 + y * (1 / 24 + y * (-1 / 720 + y * (1 / 40320 + y * (-1 / 3628800)))))
    s2 = 2.0 * sin * cos
    c2 = 1.0 - 2.0 * sin * sin
    return 1.0 - 2.0 * s2 * s2, 2.0 * s2 * c2


def fraction_of_turn(product, count, inverse):
    r = product - jnp.floor(product * inverse + 0.5) * count
    return r * inverse


def table_kernel(count, wave, table, twist_c, twist_s, weight):
    k = count[0].astype(F32)
    k_lane = jnp.maximum(jnp.full((8, 128), k, F32), 1.0)
    inverse = 1.0 / k_lane
    k1, inv1 = k_lane[0:1, 0:1], inverse[0:1, 0:1]
    m_row = wave[...].astype(F32)
    for q in range(2):
        piece = (lax.broadcasted_iota(jnp.int32, (8, MW), 0) + 8 * q).astype(F32)
        cos, sin = cos_sin_turns(fraction_of_turn(piece * m_row, k1, inv1))
        for row in range(8):
            twist_c[8 * q + row] = cos[row : row + 1]
            twist_s[8 * q + row] = sin[row : row + 1]
    top = jnp.full((8, MW), (count[0] - 1) // 2, jnp.int32)
    m8 = jnp.broadcast_to(wave[...], (8, MW))
    w = jnp.where(m8 == 0, 1.0, 2.0)
    weight[...] = jnp.where(m8 <= top, w, 0.0)
    for q in range(MW // 128):
        chunk = jnp.broadcast_to(m_row[:, 128 * q : 128 * q + 128], (128, 128))
        column = jnp.transpose(chunk, (1, 0))
        for c in range(PIECE // 128):
            x = ((lax.broadcasted_iota(jnp.int32, (128, 128), 1) + 128 * c) * PIECES).astype(F32)
            cos, sin = cos_sin_turns(fraction_of_turn(x * column, k1, inv1))
            table[128 * q : 128 * q + 128, 128 * c : 128 * c + 128] = cos.astype(BF16)
            table[MW + 128 * q : MW + 128 * q + 128, 128 * c : 128 * c + 128] = (-sin).astype(BF16)


def make_table(count, wave):
    return pl.pallas_call(
        table_kernel,
        in_specs=[pl.BlockSpec(memory_space=pltpu.SMEM), pl.BlockSpec(memory_space=pltpu.VMEM)],
        out_specs=[pl.BlockSpec(memory_space=pltpu.VMEM)] * 4,
        out_shape=[
            jax.ShapeDtypeStruct((2 * MW, PIECE), BF16),
            jax.ShapeDtypeStruct((PIECES, 1, MW), F32),
            jax.ShapeDtypeStruct((PIECES, 1, MW), F32),
            jax.ShapeDtypeStruct((8, MW), F32),
        ],
        compiler_params=pltpu.CompilerParams(vmem_limit_bytes=32 * 1024 * 1024),
        cost_estimate=pl.CostEstimate(flops=50_000_000, transcendentals=0, bytes_accessed=4_000_000),
        name="trig_table",
    )(count, wave)


PSTEP = 8
SENT = 248


def grid_kernel(count, data, table, twist_c, twist_s, weight, out, f_re, f_im, twisted):
    step = pl.program_id(0)

    @pl.when(step == 0)
    def _():
        row = lax.broadcasted_iota(jnp.int32, (192, 256), 0)
        col = lax.broadcasted_iota(jnp.int32, (192, 256), 1)
        pick_main = (col == (row % 16) * 16 + row // 16).astype(F32).astype(BF16)
        pick_rest = (col == (row % 16) * 16 + 12 + (row // 16) % 3).astype(F32).astype(BF16)
        lane = lax.broadcasted_iota(jnp.int32, (48, 128), 1) // 32
        rest = [[jnp.zeros((48, 128), F32) for _ in range(2)] for _ in range(4)]
        for a in range(8):
            x = data[16 * a : 16 * a + 16].reshape(256, 128)
            lanes = slice(128 * a, 128 * a + 128)
            w = weight[0:1, lanes]
            main = jnp.dot(pick_main, x, preferred_element_type=F32)
            f_re[:, lanes] = main[0:96] * w
            f_im[:, lanes] = main[96:192] * w
            more = jnp.dot(pick_rest, x, preferred_element_type=F32)
            for q in range(4):
                piece = more[48 * q : 48 * q + 48]
                shift = (32 * (a % 4) - 32 * q) % 128
                if shift:
                    piece = pltpu.roll(piece, shift, 1)
                rest[q][a // 4] = jnp.where(lane == a % 4, piece, rest[q][a // 4])
        for half in range(2):
            lanes = slice(1024 + 128 * half, 1152 + 128 * half)
            w = weight[0:1, lanes]
            f_re[0:48, lanes] = rest[0][half] * w
            f_re[48:96, lanes] = rest[1][half] * w
            f_im[0:48, lanes] = rest[2][half] * w
            f_im[48:96, lanes] = rest[3][half] * w

    for u in range(PSTEP):
        piece = step * PSTEP + u
        for chunk in range(MW // 128):
            lanes = slice(128 * chunk, 128 * chunk + 128)
            cos = twist_c[piece, :, lanes]
            sin = twist_s[piece, :, lanes]
            re, im = f_re[:, lanes], f_im[:, lanes]
            twisted[96 * u : 96 * u + 96, lanes] = (re * cos - im * sin).astype(BF16)
            twisted[96 * u : 96 * u + 96, MW + 128 * chunk : MW + 128 * chunk + 128] = (
                re * sin + im * cos
            ).astype(BF16)
    res = jnp.dot(twisted[...], table[...], preferred_element_type=F32)
    lon = lax.broadcasted_iota(jnp.int32, (96, PIECE), 1) * PIECES + step * PSTEP
    left = lax.broadcasted_iota(jnp.int32, (48, 128), 1) < 64
    pick_row = lax.broadcasted_iota(jnp.int32, (8, 128), 0) == 0
    pick_col = lax.broadcasted_iota(jnp.int32, (8, 128), 1) == 64
    pick = (pick_row & pick_col).astype(F32).astype(BF16)
    for u in range(PSTEP):
        keep = lon + u < count[0]
        val = jnp.where(keep, res[96 * u : 96 * u + 96], 0.0)
        out[u, 0:96] = val[:, 0:128].astype(BF16)
        out[u, 96:192] = val[:, 128:256].astype(BF16)
        rest = val[:, 256:384]
        out[u, 192:240] = jnp.where(left, rest[0:48], pltpu.roll(rest[48:96], 64, 1)).astype(BF16)
        rest = jnp.concatenate([rest, jnp.zeros((32, 128), F32)], axis=0).astype(BF16)
        last = lax.dot_general(pick, rest, NT, preferred_element_type=F32)
        out[u, 240:SENT] = last.astype(BF16)


def make_grid(count, data, tables):
    def whole(shape):
        return pl.BlockSpec(shape, lambda i: (0,) * len(shape))

    return pl.pallas_call(
        grid_kernel,
        grid=(PIECES // PSTEP,),
        in_specs=[
            pl.BlockSpec((1,), lambda i: (0,), memory_space=pltpu.SMEM),
            whole((128, 16, 128)),
            whole((2 * MW, PIECE)),
            whole((PIECES, 1, MW)),
            whole((PIECES, 1, MW)),
            whole((8, MW)),
        ],
        out_specs=pl.BlockSpec((PSTEP, SENT, 128), lambda i: (i, 0, 0)),
        out_shape=jax.ShapeDtypeStruct((PIECES, SENT, 128), BF16),
        scratch_shapes=[
            pltpu.VMEM((96, MW), F32),
            pltpu.VMEM((96, MW), F32),
            pltpu.VMEM((96 * PSTEP, 2 * MW), BF16),
        ],
        compiler_params=pltpu.CompilerParams(vmem_limit_bytes=48 * 1024 * 1024),
        name="grid_product",
    )(count, data, *tables)


def unpack_kernel(rows, out_u, out_v, out_t, wide):
    step = pl.program_id(0)
    for part in range(2):

        @pl.when(step == part)
        def _(part=part):
            for slot in range(BAND_MAX):
                chunk = rows[slot, 96 * part : 96 * part + 96]
                wide[97 * slot : 97 * slot + 96, :] = chunk.astype(F32)

    @pl.when(step == 2)
    def _():
        left = lax.broadcasted_iota(jnp.int32, (48, 128), 1) < 64
        pick_row = lax.broadcasted_iota(jnp.int32, (8, 128), 0) == 0
        pick_col = lax.broadcasted_iota(jnp.int32, (8, 128), 1) == 64
        pick = (pick_row & pick_col).astype(F32).astype(BF16)
        for slot in range(BAND_MAX):
            both = rows[slot, 192:240].astype(F32)
            last = lax.dot_general(
                rows[slot, 240:SENT], pick, (((0,), (0,)), ((), ())), preferred_element_type=F32
            )
            for half, val in enumerate((both, pltpu.roll(both, 64, 1))):
                val = jnp.where(left, val, 0.0) + last[48 * half : 48 * half + 48]
                wide[97 * slot + 48 * half : 97 * slot + 48 * half + 48, :] = val

    for lv in range(2):
        for fld, out in enumerate((out_u, out_v, out_t)):
            for src in range(16):
                row = lv * 48 + fld * 16 + src
                out[2 * src + lv] = wide[pl.ds(row, BAND_MAX, stride=97), :]


def unpack(rows):
    leaf = jax.ShapeDtypeStruct((LEVELS, BAND_MAX, PIECE), F32)
    return pl.pallas_call(
        unpack_kernel,
        grid=(PIECE // 128,),
        in_specs=[pl.BlockSpec((BAND_MAX, SENT, 128), lambda i: (0, 0, 0))],
        out_specs=[pl.BlockSpec((LEVELS, BAND_MAX, 128), lambda i: (0, 0, i))] * 3,
        out_shape=[leaf] * 3,
        scratch_shapes=[pltpu.VMEM((BAND_MAX * 97, 128), F32)],
        compiler_params=pltpu.CompilerParams(vmem_limit_bytes=24 * 1024 * 1024),
        name="unpack",
    )(rows)


def wave_row(orders):
    lower = orders[:, 0::2]
    both = jnp.stack([lower, MW - 1 - lower], axis=1)
    return jnp.concatenate([both[:, :, :KM].reshape(1, -1), both[:, :, KM:].reshape(1, -1)], axis=1)


def per_device(rot, dil, tmp, pol, orders, counts, limits):
    band = lax.axis_index("aa").astype(jnp.int32)
    slot = lax.axis_index("ba").astype(jnp.int32)
    sent = wind_legendre(rot, dil, tmp, pol, orders, limits, band[None])
    got = lax.all_to_all(sent, ("aa", "ba"), split_axis=0, concat_axis=0, tiled=True)
    edges = lax.dynamic_slice_in_dim(limits, band, 2, 0)
    lat = edges[0] + slot
    count = jnp.where(lat < edges[1], jnp.sum(jnp.where(jnp.arange(96) == lat, counts, 0)), 0)
    count = count.astype(jnp.int32)[None]
    tables = make_table(count, wave_row(orders))
    pieces = make_grid(count, got, tables)
    rows = lax.all_to_all(pieces, "ba", split_axis=0, concat_axis=0, tiled=True)
    return tuple(unpack(rows))


def solution(mesh):
    return jax.shard_map(
        per_device,
        mesh=mesh,
        in_specs=(
            P("ba", None, "aa"),
            P("ba", None, "aa"),
            P("ba", None, "aa"),
            P(None, "aa"),
            P(),
            P(),
            P(),
        ),
        out_specs=(P(None, "aa", "ba"), P(None, "aa", "ba"), P(None, "aa", "ba")),
        check_vma=False,
    )
```

```python
import functools
import math

import jax
import jax.numpy as jnp
from jax import lax
from jax.experimental import pallas as pl
from jax.experimental.pallas import tpu as pltpu
from jax.sharding import PartitionSpec as P

MW = 1280
WIDTH = MW + 1
PAIRS = 80
GROUP = 16
STEPS = PAIRS // GROUP
MAIN = GROUP * MW
WIN = 1408
LATH = 48
BAND_MAX = 16
PIECES = 16
PIECE = 384
LEVELS = 32
KM = 64
KR = PAIRS - KM
KALL = 2 * PAIRS + 1
AHEAD = 2
PITCH = 17
F32 = jnp.float32
BF16 = jnp.bfloat16
NT = (((1,), (1,)), ((), ()))


def wind_legendre_kernel(
    orders,
    limits,
    where_am_i,
    rot,
    dil,
    tmp,
    pol,
    rot_x,
    dil_x,
    tmp_x,
    pol_x,
    out,
    poly,
    fields,
    coef_a,
    coef_b,
    coef_c,
    masks,
    north,
    south,
    tiles,
    sem_f,
    sem_p,
):
    me = where_am_i[0]
    end = STEPS * MAIN

    def span(g, start, size):
        lanes = pl.ds(start, size)
        for src, ref in enumerate((rot, dil, tmp, tmp)):
            for lv in range(2):
                rows = pl.ds(4 * src + 2 * lv, 2)
                yield pltpu.make_async_copy(
                    ref.at[lv, :, lanes], fields.at[rows, lanes], sem_f.at[2 * src + lv, g]
                )
        yield pltpu.make_async_copy(pol.at[:, lanes], poly.at[:, lanes], sem_p.at[g])

    def copies(g):
        return span(g, pl.multiple_of(g * MAIN + 128, 128), MAIN)

    def first_copies():
        return span(0, 0, MAIN + 128)

    def last_copies():
        return span(STEPS - 1, (STEPS - 1) * MAIN + 128, MAIN - 128)

    for copy in first_copies():
        copy.start()
    for g in range(1, AHEAD):
        for copy in copies(g):
            copy.start()

    lane2 = lax.broadcasted_iota(jnp.int32, (2, 128), 1)
    for src, ref in enumerate((rot_x, dil_x, tmp_x, tmp_x)):
        for lv in range(2):
            edge = jnp.where(lane2 < PAIRS, ref[lv].astype(F32), 0.0).astype(BF16)
            fields[4 * src + 2 * lv : 4 * src + 2 * lv + 2, end : end + 128] = edge
    lane48 = lax.broadcasted_iota(jnp.int32, (LATH, 128), 1)
    poly[:, end : end + 128] = jnp.where(lane48 < PAIRS, pol_x[...].astype(F32), 0.0).astype(BF16)

    for copy in first_copies():
        copy.wait()

    def turn(block):
        @pl.when((block > 0) & (block < STEPS - 1))
        def _():
            for copy in copies(block):
                copy.wait()

        @pl.when(block == STEPS - 1)
        def _():
            for copy in last_copies():
                copy.wait()

        @pl.when(block + AHEAD < STEPS - 1)
        def _():
            for copy in copies(block + AHEAD):
                copy.start()

        @pl.when(block + AHEAD == STEPS - 1)
        def _():
            for copy in last_copies():
                copy.start()

    def group(step, carry):
        one_group(step, turn, me, orders, poly, fields, coef_a, coef_b, coef_c, masks, north, south)
        return carry

    lax.fori_loop(0, STEPS, group, 0)
    pack_tiles(limits, out, north, south, tiles)


def one_group(step, turn, me, orders, poly, fields, coef_a, coef_b, coef_c, masks, north, south):
    turn(step)
    origin = pl.multiple_of(step * MAIN, 128)

    lane = lax.broadcasted_iota(jnp.int32, (GROUP, WIN), 1)
    sub = lax.broadcasted_iota(jnp.int32, (GROUP, WIN), 0)
    low = [orders[me, 2 * (step * GROUP + s)] for s in range(GROUP)]
    sub1 = lax.broadcasted_iota(jnp.int32, (GROUP, 128), 0)
    lower1 = jnp.zeros((GROUP, 128), jnp.int32)
    for s in range(GROUP):
        lower1 = jnp.where(sub1 == s, low[s], lower1)
    lower = jnp.concatenate([lower1] * (WIN // 128), axis=1)
    pos = lane - sub - step * GROUP
    valid = (pos >= 0) & (pos < WIDTH)
    first = pos < MW - lower
    wave_i = jnp.where(first, lower, MW - 1 - lower)
    deg_i = jnp.where(first, lower + pos, pos - 1)
    masks[0] = jnp.where(valid & first, 1.0, 0.0)
    masks[1] = jnp.where(valid & ~first, 1.0, 0.0)
    wave = wave_i.astype(F32)
    usable = valid & (deg_i > 0)
    deg = jnp.where(usable, deg_i, 1).astype(F32)
    square = deg * deg
    eps_over_n = jnp.sqrt(
        jnp.maximum((deg - wave) * (deg + wave), 0.0) / ((4.0 * square - 1.0) * square)
    )
    eps_over_n = jnp.where(usable, eps_over_n, 0.0)
    coef_a[...] = jnp.where(deg > 1.5, eps_over_n, 0.0)
    coef_b[...] = pltpu.roll(eps_over_n, WIN - 1, 1)
    coef_c[...] = jnp.where(usable, wave / (square + deg), 0.0)

    early = step < KM // GROUP
    base = jnp.where(early, step * GROUP, 2 * KM + (step - KM // GROUP) * GROUP)
    seg_off = jnp.where(early, KM, KR)

    def wide(tile):
        return jnp.concatenate([tile] * (WIN // 128), axis=1)

    row8 = lax.broadcasted_iota(jnp.int32, (8, 128), 0)
    row_even = wide((row8 & 1) == 0)
    sign = wide(jnp.where(((row8 & 1) == 0) == (row8 < 4), 1.0, -1.0))
    row16 = lax.broadcasted_iota(jnp.int32, (16, 128), 0)
    lane16 = lax.broadcasted_iota(jnp.int32, (16, 128), 1)
    alternate = jnp.where((lane16 & 1) == 0, 1.0, -1.0)
    flip_wind = wide(alternate.astype(BF16))
    flip_heat = wide(jnp.where(row16 % 8 < 4, 1.0, alternate).astype(BF16))

    def spread(ref, s):
        return ref[pl.ds(s, 8, stride=0), :]

    results = []
    for s in range(GROUP):
        window = pl.ds(pl.multiple_of(origin + s * MW, 128), WIN)
        both = fields[:, window].astype(F32)
        x, heat = both[0:8], both[8:16]
        other = jnp.where(row_even, pltpu.roll(x, 3, 0), pltpu.roll(x, 5, 0))
        wind = (
            spread(coef_b, s) * pltpu.roll(x, WIN - 1, 1)
            - spread(coef_a, s) * pltpu.roll(x, 1, 1)
            + spread(coef_c, s) * (other * sign)
        )
        m0, m1 = spread(masks.at[0], s), spread(masks.at[1], s)
        winds = jnp.concatenate([wind * m0, wind * m1], axis=0).astype(BF16)
        heats = jnp.concatenate([heat * m0, heat * m1], axis=0).astype(BF16)
        data = jnp.concatenate([winds, winds * flip_wind, heats * flip_heat], axis=0)
        results.append(lax.dot_general(data, poly[:, window], NT, preferred_element_type=F32))
    for s, res in enumerate(results):
        pair = step * GROUP + s
        odd = (pair & 1, (pair + low[s]) & 1)
        for seg in range(2):
            at = base + s + seg * seg_off
            factor = (1 - 2 * odd[seg]).astype(F32)
            north[pl.ds(at, 8, stride=KALL), :] = res[seg * 8 : seg * 8 + 8]
            south[pl.ds(at, 8, stride=KALL), :] = res[16 + seg * 8 : 24 + seg * 8] * factor
            heat = res[32 + seg * 8 : 40 + seg * 8]
            north[pl.ds(8 * KALL + at, 4, stride=KALL), :] = heat[0:4]
            south[pl.ds(8 * KALL + at, 4, stride=KALL), :] = heat[4:8] * factor


def pack_tiles(limits, out, north, south, tiles):
    dest = lax.broadcasted_iota(jnp.int32, (128, LATH), 0)
    column = lax.broadcasted_iota(jnp.int32, (128, LATH), 1)
    lat = dest % BAND_MAX
    for band in range(8):
        lat = lat + jnp.where(dest // BAND_MAX == band, limits[band], 0)
    pick_n = (lat == column).astype(F32).astype(BF16)
    pick_s = (2 * LATH - 1 - lat == column).astype(F32).astype(BF16)

    def rows_of(ref, part, lv, fld, start, size):
        row = fld * 4 + lv * 2 + part
        val = ref[row * KALL + start : row * KALL + start + size, :]
        return (-val if fld == 1 else val).astype(BF16)

    def select(rows_n, rows_s, row):
        val = lax.dot_general(pick_n, rows_n, NT, preferred_element_type=F32)
        val = val + lax.dot_general(pick_s, rows_s, NT, preferred_element_type=F32)
        for block in range(16):
            tiles[pl.ds(row + 8 * PITCH * block, 8, stride=PITCH), :] = val[8 * block : 8 * block + 8]

    for part in range(2):
        for lv in range(2):
            for fld in range(3):
                select(
                    rows_of(north, part, lv, fld, 0, 2 * KM),
                    rows_of(south, part, lv, fld, 0, 2 * KM),
                    part * 6 + lv * 3 + fld,
                )
    for fld in range(3):
        both = []
        for ref in (north, south):
            both.append(
                jnp.concatenate(
                    [rows_of(ref, q // 2, q % 2, fld, 2 * KM, 2 * KR) for q in range(4)],
                    axis=0,
                )
            )
        select(both[0], both[1], 12 + fld)
    for block in range(16):
        tiles[pl.ds(15 + 8 * PITCH * block, 8, stride=PITCH), :] = jnp.zeros((8, 128), F32)
    for block in range(16):
        for dst in range(8 * block, 8 * block + 8):
            out[dst] = tiles[PITCH * dst : PITCH * dst + 16, :].astype(BF16)


def wind_legendre(rot, dil, tmp, pol, orders, limits, me):
    rot, dil, tmp, pol, orders, limits = (
        pltpu.with_memory_space_constraint(v, pltpu.HBM) for v in (rot, dil, tmp, pol, orders, limits)
    )
    smem = pl.BlockSpec(memory_space=pltpu.SMEM)
    hbm = pl.BlockSpec(memory_space=pltpu.HBM)
    tail = pl.BlockSpec((2, 2, 128), lambda i: (0, 0, PAIRS * MW // 128))
    return pl.pallas_call(
        wind_legendre_kernel,
        grid=(1,),
        in_specs=[
            smem,
            smem,
            smem,
            hbm,
            hbm,
            hbm,
            hbm,
            tail,
            tail,
            tail,
            pl.BlockSpec((LATH, 128), lambda i: (0, PAIRS * MW // 128)),
        ],
        out_specs=pl.BlockSpec((128, 16, 128), lambda i: (0, 0, 0)),
        out_shape=jax.ShapeDtypeStruct((128, 16, 128), BF16),
        scratch_shapes=[
            pltpu.VMEM((LATH, STEPS * MAIN + 128), BF16),
            pltpu.VMEM((16, STEPS * MAIN + 128), BF16),
            pltpu.VMEM((GROUP, WIN), F32),
            pltpu.VMEM((GROUP, WIN), F32),
            pltpu.VMEM((GROUP, WIN), F32),
            pltpu.VMEM((2, GROUP, WIN), F32),
            pltpu.VMEM((12 * KALL, LATH), F32),
            pltpu.VMEM((12 * KALL, LATH), F32),
            pltpu.VMEM((128 * PITCH, 128), F32),
            pltpu.SemaphoreType.DMA((8, STEPS)),
            pltpu.SemaphoreType.DMA((STEPS,)),
        ],
        compiler_params=pltpu.CompilerParams(vmem_limit_bytes=40 * 1024 * 1024),
        name="wind_legendre",
    )(orders, limits, me, rot, dil, tmp, pol, rot, dil, tmp, pol)


def cos_sin_turns(turns):
    z = turns * (math.pi / 2.0)
    y = z * z
    sin = z * (1.0 + y * (-1 / 6 + y * (1 / 120 + y * (-1 / 5040 + y * (1 / 362880)))))
    cos = 1.0 + y * (-1 / 2 + y * (1 / 24 + y * (-1 / 720 + y * (1 / 40320 + y * (-1 / 3628800)))))
    s2 = 2.0 * sin * cos
    c2 = 1.0 - 2.0 * sin * sin
    return 1.0 - 2.0 * s2 * s2, 2.0 * s2 * c2


def fraction_of_turn(product, count, inverse):
    r = product - jnp.floor(product * inverse + 0.5) * count
    return r * inverse


def table_kernel(count, wave, table, twist_c, twist_s, weight):
    k = count[0].astype(F32)
    k_lane = jnp.maximum(jnp.full((8, 128), k, F32), 1.0)
    inverse = 1.0 / k_lane
    k1, inv1 = k_lane[0:1, 0:1], inverse[0:1, 0:1]
    m_row = wave[...].astype(F32)
    for q in range(2):
        piece = (lax.broadcasted_iota(jnp.int32, (8, MW), 0) + 8 * q).astype(F32)
        cos, sin = cos_sin_turns(fraction_of_turn(piece * m_row, k1, inv1))
        for row in range(8):
            twist_c[8 * q + row] = cos[row : row + 1]
            twist_s[8 * q + row] = sin[row : row + 1]
    top = jnp.full((8, MW), (count[0] - 1) // 2, jnp.int32)
    m8 = jnp.broadcast_to(wave[...], (8, MW))
    w = jnp.where(m8 == 0, 1.0, 2.0)
    weight[...] = jnp.where(m8 <= top, w, 0.0)
    for q in range(MW // 128):
        chunk = jnp.broadcast_to(m_row[:, 128 * q : 128 * q + 128], (128, 128))
        column = jnp.transpose(chunk, (1, 0))
        for c in range(PIECE // 128):
            x = ((lax.broadcasted_iota(jnp.int32, (128, 128), 1) + 128 * c) * PIECES).astype(F32)
            cos, sin = cos_sin_turns(fraction_of_turn(x * column, k1, inv1))
            table[128 * q : 128 * q + 128, 128 * c : 128 * c + 128] = cos.astype(BF16)
            table[MW + 128 * q : MW + 128 * q + 128, 128 * c : 128 * c + 128] = (-sin).astype(BF16)


def make_table(count, wave):
    return pl.pallas_call(
        table_kernel,
        in_specs=[pl.BlockSpec(memory_space=pltpu.SMEM), pl.BlockSpec(memory_space=pltpu.VMEM)],
        out_specs=[pl.BlockSpec(memory_space=pltpu.VMEM)] * 4,
        out_shape=[
            jax.ShapeDtypeStruct((2 * MW, PIECE), BF16),
            jax.ShapeDtypeStruct((PIECES, 1, MW), F32),
            jax.ShapeDtypeStruct((PIECES, 1, MW), F32),
            jax.ShapeDtypeStruct((8, MW), F32),
        ],
        compiler_params=pltpu.CompilerParams(vmem_limit_bytes=32 * 1024 * 1024),
        cost_estimate=pl.CostEstimate(flops=50_000_000, transcendentals=0, bytes_accessed=4_000_000),
        name="trig_table",
    )(count, wave)


PSTEP = 8
SENT = 248


def grid_kernel(count, data, table, twist_c, twist_s, weight, out, f_re, f_im, twisted):
    step = pl.program_id(0)

    @pl.when(step == 0)
    def _():
        row = lax.broadcasted_iota(jnp.int32, (192, 256), 0)
        col = lax.broadcasted_iota(jnp.int32, (192, 256), 1)
        pick_main = (col == (row % 16) * 16 + row // 16).astype(F32).astype(BF16)
        pick_rest = (col == (row % 16) * 16 + 12 + (row // 16) % 3).astype(F32).astype(BF16)
        lane = lax.broadcasted_iota(jnp.int32, (48, 128), 1) // 32
        rest = [[jnp.zeros((48, 128), F32) for _ in range(2)] for _ in range(4)]
        for a in range(8):
            x = data[16 * a : 16 * a + 16].reshape(256, 128)
            lanes = slice(128 * a, 128 * a + 128)
            w = weight[0:1, lanes]
            main = jnp.dot(pick_main, x, preferred_element_type=F32)
            f_re[:, lanes] = main[0:96] * w
            f_im[:, lanes] = main[96:192] * w
            more = jnp.dot(pick_rest, x, preferred_element_type=F32)
            for q in range(4):
                piece = more[48 * q : 48 * q + 48]
                shift = (32 * (a % 4) - 32 * q) % 128
                if shift:
                    piece = pltpu.roll(piece, shift, 1)
                rest[q][a // 4] = jnp.where(lane == a % 4, piece, rest[q][a // 4])
        for half in range(2):
            lanes = slice(1024 + 128 * half, 1152 + 128 * half)
            w = weight[0:1, lanes]
            f_re[0:48, lanes] = rest[0][half] * w
            f_re[48:96, lanes] = rest[1][half] * w
            f_im[0:48, lanes] = rest[2][half] * w
            f_im[48:96, lanes] = rest[3][half] * w

    for u in range(PSTEP):
        piece = step * PSTEP + u
        for chunk in range(MW // 128):
            lanes = slice(128 * chunk, 128 * chunk + 128)
            cos = twist_c[piece, :, lanes]
            sin = twist_s[piece, :, lanes]
            re, im = f_re[:, lanes], f_im[:, lanes]
            twisted[96 * u : 96 * u + 96, lanes] = (re * cos - im * sin).astype(BF16)
            twisted[96 * u : 96 * u + 96, MW + 128 * chunk : MW + 128 * chunk + 128] = (
                re * sin + im * cos
            ).astype(BF16)
    res = jnp.dot(twisted[...], table[...], preferred_element_type=F32)
    lon = lax.broadcasted_iota(jnp.int32, (96, PIECE), 1) * PIECES + step * PSTEP
    left = lax.broadcasted_iota(jnp.int32, (48, 128), 1) < 64
    pick_row = lax.broadcasted_iota(jnp.int32, (8, 128), 0) == 0
    pick_col = lax.broadcasted_iota(jnp.int32, (8, 128), 1) == 64
    pick = (pick_row & pick_col).astype(F32).astype(BF16)
    for u in range(PSTEP):
        keep = lon + u < count[0]
        val = jnp.where(keep, res[96 * u : 96 * u + 96], 0.0)
        out[u, 0:96] = val[:, 0:128].astype(BF16)
        out[u, 96:192] = val[:, 128:256].astype(BF16)
        rest = val[:, 256:384]
        out[u, 192:240] = jnp.where(left, rest[0:48], pltpu.roll(rest[48:96], 64, 1)).astype(BF16)
        rest = jnp.concatenate([rest, jnp.zeros((32, 128), F32)], axis=0).astype(BF16)
        last = lax.dot_general(pick, rest, NT, preferred_element_type=F32)
        out[u, 240:SENT] = last.astype(BF16)


def make_grid(count, data, tables):
    def whole(shape):
        return pl.BlockSpec(shape, lambda i: (0,) * len(shape))

    return pl.pallas_call(
        grid_kernel,
        grid=(PIECES // PSTEP,),
        in_specs=[
            pl.BlockSpec((1,), lambda i: (0,), memory_space=pltpu.SMEM),
            whole((128, 16, 128)),
            whole((2 * MW, PIECE)),
            whole((PIECES, 1, MW)),
            whole((PIECES, 1, MW)),
            whole((8, MW)),
        ],
        out_specs=pl.BlockSpec((PSTEP, SENT, 128), lambda i: (i, 0, 0)),
        out_shape=jax.ShapeDtypeStruct((PIECES, SENT, 128), BF16),
        scratch_shapes=[
            pltpu.VMEM((96, MW), F32),
            pltpu.VMEM((96, MW), F32),
            pltpu.VMEM((96 * PSTEP, 2 * MW), BF16),
        ],
        compiler_params=pltpu.CompilerParams(vmem_limit_bytes=48 * 1024 * 1024),
        name="grid_product",
    )(count, data, *tables)


def unpack_kernel(rows, out_u, out_v, out_t, wide):
    step = pl.program_id(0)
    for part in range(2):

        @pl.when(step == part)
        def _(part=part):
            for slot in range(BAND_MAX):
                chunk = rows[slot, 96 * part : 96 * part + 96]
                wide[97 * slot : 97 * slot + 96, :] = chunk.astype(F32)

    @pl.when(step == 2)
    def _():
        left = lax.broadcasted_iota(jnp.int32, (48, 128), 1) < 64
        pick_row = lax.broadcasted_iota(jnp.int32, (8, 128), 0) == 0
        pick_col = lax.broadcasted_iota(jnp.int32, (8, 128), 1) == 64
        pick = (pick_row & pick_col).astype(F32).astype(BF16)
        for slot in range(BAND_MAX):
            both = rows[slot, 192:240].astype(F32)
            last = lax.dot_general(
                rows[slot, 240:SENT], pick, (((0,), (0,)), ((), ())), preferred_element_type=F32
            )
            for half, val in enumerate((both, pltpu.roll(both, 64, 1))):
                val = jnp.where(left, val, 0.0) + last[48 * half : 48 * half + 48]
                wide[97 * slot + 48 * half : 97 * slot + 48 * half + 48, :] = val

    for lv in range(2):
        for fld, out in enumerate((out_u, out_v, out_t)):
            for src in range(16):
                row = lv * 48 + fld * 16 + src
                out[2 * src + lv] = wide[pl.ds(row, BAND_MAX, stride=97), :]


def unpack(rows):
    leaf = jax.ShapeDtypeStruct((LEVELS, BAND_MAX, PIECE), F32)
    return pl.pallas_call(
        unpack_kernel,
        grid=(PIECE // 128,),
        in_specs=[pl.BlockSpec((BAND_MAX, SENT, 128), lambda i: (0, 0, 0))],
        out_specs=[pl.BlockSpec((LEVELS, BAND_MAX, 128), lambda i: (0, 0, i))] * 3,
        out_shape=[leaf] * 3,
        scratch_shapes=[pltpu.VMEM((BAND_MAX * 97, 128), F32)],
        compiler_params=pltpu.CompilerParams(vmem_limit_bytes=24 * 1024 * 1024),
        name="unpack",
    )(rows)


def wave_row(orders):
    lower = orders[:, 0::2]
    both = jnp.stack([lower, MW - 1 - lower], axis=1)
    return jnp.concatenate([both[:, :, :KM].reshape(1, -1), both[:, :, KM:].reshape(1, -1)], axis=1)


def per_device(rot, dil, tmp, pol, orders, counts, limits):
    band = lax.axis_index("aa").astype(jnp.int32)
    slot = lax.axis_index("ba").astype(jnp.int32)
    sent = wind_legendre(rot, dil, tmp, pol, orders, limits, band[None])
    got = lax.all_to_all(sent, ("aa", "ba"), split_axis=0, concat_axis=0, tiled=True)
    edges = lax.dynamic_slice_in_dim(limits, band, 2, 0)
    lat = edges[0] + slot
    count = jnp.where(lat < edges[1], jnp.sum(jnp.where(jnp.arange(96) == lat, counts, 0)), 0)
    count = count.astype(jnp.int32)[None]
    tables = make_table(count, wave_row(orders))
    pieces = make_grid(count, got, tables)
    rows = lax.all_to_all(pieces, "ba", split_axis=0, concat_axis=0, tiled=True)
    return tuple(unpack(rows))


def solution(mesh):
    return jax.shard_map(
        per_device,
        mesh=mesh,
        in_specs=(
            P("ba", None, "aa"),
            P("ba", None, "aa"),
            P("ba", None, "aa"),
            P(None, "aa"),
            P(),
            P(),
            P(),
        ),
        out_specs=(P(None, "aa", "ba"), P(None, "aa", "ba"), P(None, "aa", "ba")),
        check_vma=False,
    )
```

```python
import functools
import math

import jax
import jax.numpy as jnp
from jax import lax
from jax.experimental import pallas as pl
from jax.experimental.pallas import tpu as pltpu
from jax.sharding import PartitionSpec as P

MW = 1280
WIDTH = MW + 1
PAIRS = 80
GROUP = 16
STEPS = PAIRS // GROUP
MAIN = GROUP * MW
WIN = 1408
LATH = 48
BAND_MAX = 16
PIECES = 16
PIECE = 384
LEVELS = 32
KM = 64
KR = PAIRS - KM
KALL = 2 * PAIRS + 1
AHEAD = 2
F32 = jnp.float32
BF16 = jnp.bfloat16
NT = (((1,), (1,)), ((), ()))


def wind_legendre_kernel(
    orders,
    limits,
    where_am_i,
    rot,
    dil,
    tmp,
    pol,
    rot_x,
    dil_x,
    tmp_x,
    pol_x,
    out,
    poly,
    fields,
    coef_a,
    coef_b,
    coef_c,
    masks,
    north,
    south,
    tiles,
    sem_f,
    sem_p,
):
    me = where_am_i[0]
    end = STEPS * MAIN

    def span(g, start, size):
        lanes = pl.ds(start, size)
        for src, ref in enumerate((rot, dil, tmp, tmp)):
            for lv in range(2):
                rows = pl.ds(4 * src + 2 * lv, 2)
                yield pltpu.make_async_copy(
                    ref.at[lv, :, lanes], fields.at[rows, lanes], sem_f.at[2 * src + lv, g]
                )
        yield pltpu.make_async_copy(pol.at[:, lanes], poly.at[:, lanes], sem_p.at[g])

    def copies(g):
        return span(g, pl.multiple_of(g * MAIN + 128, 128), MAIN)

    def first_copies():
        return span(0, 0, MAIN + 128)

    def last_copies():
        return span(STEPS - 1, (STEPS - 1) * MAIN + 128, MAIN - 128)

    for copy in first_copies():
        copy.start()
    for g in range(1, AHEAD):
        for copy in copies(g):
            copy.start()

    lane2 = lax.broadcasted_iota(jnp.int32, (2, 128), 1)
    for src, ref in enumerate((rot_x, dil_x, tmp_x, tmp_x)):
        for lv in range(2):
            edge = jnp.where(lane2 < PAIRS, ref[lv].astype(F32), 0.0).astype(BF16)
            fields[4 * src + 2 * lv : 4 * src + 2 * lv + 2, end : end + 128] = edge
    lane48 = lax.broadcasted_iota(jnp.int32, (LATH, 128), 1)
    poly[:, end : end + 128] = jnp.where(lane48 < PAIRS, pol_x[...].astype(F32), 0.0).astype(BF16)

    for copy in first_copies():
        copy.wait()

    def turn(block):
        @pl.when((block > 0) & (block < STEPS - 1))
        def _():
            for copy in copies(block):
                copy.wait()

        @pl.when(block == STEPS - 1)
        def _():
            for copy in last_copies():
                copy.wait()

        @pl.when(block + AHEAD < STEPS - 1)
        def _():
            for copy in copies(block + AHEAD):
                copy.start()

        @pl.when(block + AHEAD == STEPS - 1)
        def _():
            for copy in last_copies():
                copy.start()

    def group(step, carry):
        one_group(step, turn, me, orders, poly, fields, coef_a, coef_b, coef_c, masks, north, south)
        return carry

    lax.fori_loop(0, STEPS, group, 0)
    pack_tiles(limits, out, north, south, tiles)


def one_group(step, turn, me, orders, poly, fields, coef_a, coef_b, coef_c, masks, north, south):
    turn(step)
    origin = pl.multiple_of(step * MAIN, 128)

    lane = lax.broadcasted_iota(jnp.int32, (GROUP, WIN), 1)
    sub = lax.broadcasted_iota(jnp.int32, (GROUP, WIN), 0)
    low = [orders[me, 2 * (step * GROUP + s)] for s in range(GROUP)]
    sub1 = lax.broadcasted_iota(jnp.int32, (GROUP, 128), 0)
    lower1 = jnp.zeros((GROUP, 128), jnp.int32)
    for s in range(GROUP):
        lower1 = jnp.where(sub1 == s, low[s], lower1)
    lower = jnp.concatenate([lower1] * (WIN // 128), axis=1)
    pos = lane - sub - step * GROUP
    valid = (pos >= 0) & (pos < WIDTH)
    first = pos < MW - lower
    wave_i = jnp.where(first, lower, MW - 1 - lower)
    deg_i = jnp.where(first, lower + pos, pos - 1)
    masks[0] = jnp.where(valid & first, 1.0, 0.0)
    masks[1] = jnp.where(valid & ~first, 1.0, 0.0)
    wave = wave_i.astype(F32)
    usable = valid & (deg_i > 0)
    deg = jnp.where(usable, deg_i, 1).astype(F32)
    square = deg * deg
    eps_over_n = jnp.sqrt(
        jnp.maximum((deg - wave) * (deg + wave), 0.0) / ((4.0 * square - 1.0) * square)
    )
    eps_over_n = jnp.where(usable, eps_over_n, 0.0)
    coef_a[...] = jnp.where(deg > 1.5, eps_over_n, 0.0)
    coef_b[...] = pltpu.roll(eps_over_n, WIN - 1, 1)
    coef_c[...] = jnp.where(usable, wave / (square + deg), 0.0)

    early = step < KM // GROUP
    base = jnp.where(early, step * GROUP, 2 * KM + (step - KM // GROUP) * GROUP)
    seg_off = jnp.where(early, KM, KR)

    def wide(tile):
        return jnp.concatenate([tile] * (WIN // 128), axis=1)

    row8 = lax.broadcasted_iota(jnp.int32, (8, 128), 0)
    row_even = wide((row8 & 1) == 0)
    sign = wide(jnp.where(((row8 & 1) == 0) == (row8 < 4), 1.0, -1.0))
    row16 = lax.broadcasted_iota(jnp.int32, (16, 128), 0)
    lane16 = lax.broadcasted_iota(jnp.int32, (16, 128), 1)
    alternate = jnp.where((lane16 & 1) == 0, 1.0, -1.0)
    flip_wind = wide(alternate.astype(BF16))
    flip_heat = wide(jnp.where(row16 % 8 < 4, 1.0, alternate).astype(BF16))

    def spread(ref, s):
        return ref[pl.ds(s, 8, stride=0), :]

    results = []
    for s in range(GROUP):
        window = pl.ds(pl.multiple_of(origin + s * MW, 128), WIN)
        both = fields[:, window].astype(F32)
        x, heat = both[0:8], both[8:16]
        other = jnp.where(row_even, pltpu.roll(x, 3, 0), pltpu.roll(x, 5, 0))
        wind = (
            spread(coef_b, s) * pltpu.roll(x, WIN - 1, 1)
            - spread(coef_a, s) * pltpu.roll(x, 1, 1)
            + spread(coef_c, s) * (other * sign)
        )
        m0, m1 = spread(masks.at[0], s), spread(masks.at[1], s)
        winds = jnp.concatenate([wind * m0, wind * m1], axis=0).astype(BF16)
        heats = jnp.concatenate([heat * m0, heat * m1], axis=0).astype(BF16)
        data = jnp.concatenate([winds, winds * flip_wind, heats * flip_heat], axis=0)
        results.append(lax.dot_general(data, poly[:, window], NT, preferred_element_type=F32))
    for s, res in enumerate(results):
        pair = step * GROUP + s
        odd = (pair & 1, (pair + low[s]) & 1)
        for seg in range(2):
            at = base + s + seg * seg_off
            factor = (1 - 2 * odd[seg]).astype(F32)
            north[pl.ds(at, 8, stride=KALL), :] = res[seg * 8 : seg * 8 + 8]
            south[pl.ds(at, 8, stride=KALL), :] = res[16 + seg * 8 : 24 + seg * 8] * factor
            heat = res[32 + seg * 8 : 40 + seg * 8]
            north[pl.ds(8 * KALL + at, 4, stride=KALL), :] = heat[0:4]
            south[pl.ds(8 * KALL + at, 4, stride=KALL), :] = heat[4:8] * factor


def pack_tiles(limits, out, north, south, tiles):
    dest = lax.broadcasted_iota(jnp.int32, (128, LATH), 0)
    column = lax.broadcasted_iota(jnp.int32, (128, LATH), 1)
    lat = dest % BAND_MAX
    for band in range(8):
        lat = lat + jnp.where(dest // BAND_MAX == band, limits[band], 0)
    pick_n = (lat == column).astype(F32).astype(BF16)
    pick_s = (2 * LATH - 1 - lat == column).astype(F32).astype(BF16)

    def rows_of(ref, part, lv, fld, start, size):
        row = fld * 4 + lv * 2 + part
        val = ref[row * KALL + start : row * KALL + start + size, :]
        return (-val if fld == 1 else val).astype(BF16)

    def select(rows_n, rows_s, row):
        val = lax.dot_general(pick_n, rows_n, NT, preferred_element_type=F32)
        val = val + lax.dot_general(pick_s, rows_s, NT, preferred_element_type=F32)
        for block in range(16):
            tiles[pl.ds(row + 128 * block, 8, stride=16), :] = val[8 * block : 8 * block + 8]

    for part in range(2):
        for lv in range(2):
            for fld in range(3):
                select(
                    rows_of(north, part, lv, fld, 0, 2 * KM),
                    rows_of(south, part, lv, fld, 0, 2 * KM),
                    part * 6 + lv * 3 + fld,
                )
    for fld in range(3):
        both = []
        for ref in (north, south):
            both.append(
                jnp.concatenate(
                    [rows_of(ref, q // 2, q % 2, fld, 2 * KM, 2 * KR) for q in range(4)],
                    axis=0,
                )
            )
        select(both[0], both[1], 12 + fld)
    for block in range(16):
        tiles[pl.ds(15 + 128 * block, 8, stride=16), :] = jnp.zeros((8, 128), F32)
    for block in range(16):
        part = tiles[128 * block : 128 * block + 128, :]
        out[8 * block : 8 * block + 8] = part.reshape(8, 16, 128).astype(BF16)


def wind_legendre(rot, dil, tmp, pol, orders, limits, me):
    rot, dil, tmp, pol, orders, limits = (
        pltpu.with_memory_space_constraint(v, pltpu.HBM) for v in (rot, dil, tmp, pol, orders, limits)
    )
    smem = pl.BlockSpec(memory_space=pltpu.SMEM)
    hbm = pl.BlockSpec(memory_space=pltpu.HBM)
    tail = pl.BlockSpec((2, 2, 128), lambda i: (0, 0, PAIRS * MW // 128))
    return pl.pallas_call(
        wind_legendre_kernel,
        grid=(1,),
        in_specs=[
            smem,
            smem,
            smem,
            hbm,
            hbm,
            hbm,
            hbm,
            tail,
            tail,
            tail,
            pl.BlockSpec((LATH, 128), lambda i: (0, PAIRS * MW // 128)),
        ],
        out_specs=pl.BlockSpec((128, 16, 128), lambda i: (0, 0, 0)),
        out_shape=jax.ShapeDtypeStruct((128, 16, 128), BF16),
        scratch_shapes=[
            pltpu.VMEM((LATH, STEPS * MAIN + 128), BF16),
            pltpu.VMEM((16, STEPS * MAIN + 128), BF16),
            pltpu.VMEM((GROUP, WIN), F32),
            pltpu.VMEM((GROUP, WIN), F32),
            pltpu.VMEM((GROUP, WIN), F32),
            pltpu.VMEM((2, GROUP, WIN), F32),
            pltpu.VMEM((12 * KALL, LATH), F32),
            pltpu.VMEM((12 * KALL, LATH), F32),
            pltpu.VMEM((2048, 128), F32),
            pltpu.SemaphoreType.DMA((8, STEPS)),
            pltpu.SemaphoreType.DMA((STEPS,)),
        ],
        compiler_params=pltpu.CompilerParams(vmem_limit_bytes=40 * 1024 * 1024),
        name="wind_legendre",
    )(orders, limits, me, rot, dil, tmp, pol, rot, dil, tmp, pol)


def cos_sin_turns(turns):
    z = turns * (math.pi / 2.0)
    y = z * z
    sin = z * (1.0 + y * (-1 / 6 + y * (1 / 120 + y * (-1 / 5040 + y * (1 / 362880)))))
    cos = 1.0 + y * (-1 / 2 + y * (1 / 24 + y * (-1 / 720 + y * (1 / 40320 + y * (-1 / 3628800)))))
    s2 = 2.0 * sin * cos
    c2 = 1.0 - 2.0 * sin * sin
    return 1.0 - 2.0 * s2 * s2, 2.0 * s2 * c2


def fraction_of_turn(product, count, inverse):
    r = product - jnp.floor(product * inverse + 0.5) * count
    return r * inverse


def table_kernel(count, wave, table, twist_c, twist_s, weight):
    k = count[0].astype(F32)
    k_lane = jnp.maximum(jnp.full((8, 128), k, F32), 1.0)
    inverse = 1.0 / k_lane
    k1, inv1 = k_lane[0:1, 0:1], inverse[0:1, 0:1]
    m_row = wave[...].astype(F32)
    for q in range(2):
        piece = (lax.broadcasted_iota(jnp.int32, (8, MW), 0) + 8 * q).astype(F32)
        cos, sin = cos_sin_turns(fraction_of_turn(piece * m_row, k1, inv1))
        for row in range(8):
            twist_c[8 * q + row] = cos[row : row + 1]
            twist_s[8 * q + row] = sin[row : row + 1]
    top = jnp.full((8, MW), (count[0] - 1) // 2, jnp.int32)
    m8 = jnp.broadcast_to(wave[...], (8, MW))
    w = jnp.where(m8 == 0, 1.0, 2.0)
    weight[...] = jnp.where(m8 <= top, w, 0.0)
    for q in range(MW // 128):
        chunk = jnp.broadcast_to(m_row[:, 128 * q : 128 * q + 128], (128, 128))
        column = jnp.transpose(chunk, (1, 0))
        for c in range(PIECE // 128):
            x = ((lax.broadcasted_iota(jnp.int32, (128, 128), 1) + 128 * c) * PIECES).astype(F32)
            cos, sin = cos_sin_turns(fraction_of_turn(x * column, k1, inv1))
            table[128 * q : 128 * q + 128, 128 * c : 128 * c + 128] = cos.astype(BF16)
            table[MW + 128 * q : MW + 128 * q + 128, 128 * c : 128 * c + 128] = (-sin).astype(BF16)


def make_table(count, wave):
    return pl.pallas_call(
        table_kernel,
        in_specs=[pl.BlockSpec(memory_space=pltpu.SMEM), pl.BlockSpec(memory_space=pltpu.VMEM)],
        out_specs=[pl.BlockSpec(memory_space=pltpu.VMEM)] * 4,
        out_shape=[
            jax.ShapeDtypeStruct((2 * MW, PIECE), BF16),
            jax.ShapeDtypeStruct((PIECES, 1, MW), F32),
            jax.ShapeDtypeStruct((PIECES, 1, MW), F32),
            jax.ShapeDtypeStruct((8, MW), F32),
        ],
        compiler_params=pltpu.CompilerParams(vmem_limit_bytes=32 * 1024 * 1024),
        cost_estimate=pl.CostEstimate(flops=50_000_000, transcendentals=0, bytes_accessed=4_000_000),
        name="trig_table",
    )(count, wave)


PSTEP = 8
SENT = 248


def grid_kernel(count, data, table, twist_c, twist_s, weight, out, f_re, f_im, twisted):
    step = pl.program_id(0)

    @pl.when(step == 0)
    def _():
        row = lax.broadcasted_iota(jnp.int32, (192, 256), 0)
        col = lax.broadcasted_iota(jnp.int32, (192, 256), 1)
        pick_main = (col == (row % 16) * 16 + row // 16).astype(F32).astype(BF16)
        pick_rest = (col == (row % 16) * 16 + 12 + (row // 16) % 3).astype(F32).astype(BF16)
        picks = jnp.concatenate([pick_main, pick_rest], axis=0)
        lane = lax.broadcasted_iota(jnp.int32, (48, 128), 1) // 32
        rest = [[jnp.zeros((48, 128), F32) for _ in range(2)] for _ in range(4)]
        for a in range(8):
            x = data[16 * a : 16 * a + 16].reshape(256, 128)
            lanes = slice(128 * a, 128 * a + 128)
            w = weight[0:1, lanes]
            picked = jnp.dot(picks, x, preferred_element_type=F32)
            main, more = picked[0:192], picked[192:384]
            f_re[:, lanes] = main[0:96] * w
            f_im[:, lanes] = main[96:192] * w
            for q in range(4):
                piece = more[48 * q : 48 * q + 48]
                shift = (32 * (a % 4) - 32 * q) % 128
                if shift:
                    piece = pltpu.roll(piece, shift, 1)
                rest[q][a // 4] = jnp.where(lane == a % 4, piece, rest[q][a // 4])
        for half in range(2):
            lanes = slice(1024 + 128 * half, 1152 + 128 * half)
            w = weight[0:1, lanes]
            f_re[0:48, lanes] = rest[0][half] * w
            f_re[48:96, lanes] = rest[1][half] * w
            f_im[0:48, lanes] = rest[2][half] * w
            f_im[48:96, lanes] = rest[3][half] * w

    for u in range(PSTEP):
        piece = step * PSTEP + u
        for chunk in range(MW // 128):
            lanes = slice(128 * chunk, 128 * chunk + 128)
            cos = twist_c[piece, :, lanes]
            sin = twist_s[piece, :, lanes]
            re, im = f_re[:, lanes], f_im[:, lanes]
            twisted[96 * u : 96 * u + 96, lanes] = (re * cos - im * sin).astype(BF16)
            twisted[96 * u : 96 * u + 96, MW + 128 * chunk : MW + 128 * chunk + 128] = (
                re * sin + im * cos
            ).astype(BF16)
    res = jnp.dot(twisted[...], table[...], preferred_element_type=F32)
    lon = lax.broadcasted_iota(jnp.int32, (96, PIECE), 1) * PIECES + step * PSTEP
    left = lax.broadcasted_iota(jnp.int32, (48, 128), 1) < 64
    pick_row = lax.broadcasted_iota(jnp.int32, (8, 128), 0) == 0
    pick_col = lax.broadcasted_iota(jnp.int32, (8, 128), 1) == 64
    pick = (pick_row & pick_col).astype(F32).astype(BF16)
    for u in range(PSTEP):
        keep = lon + u < count[0]
        val = jnp.where(keep, res[96 * u : 96 * u + 96], 0.0)
        out[u, 0:96] = val[:, 0:128].astype(BF16)
        out[u, 96:192] = val[:, 128:256].astype(BF16)
        rest = val[:, 256:384]
        out[u, 192:240] = jnp.where(left, rest[0:48], pltpu.roll(rest[48:96], 64, 1)).astype(BF16)
        rest = jnp.concatenate([rest, jnp.zeros((32, 128), F32)], axis=0).astype(BF16)
        last = lax.dot_general(pick, rest, NT, preferred_element_type=F32)
        out[u, 240:SENT] = last.astype(BF16)


def make_grid(count, data, tables):
    def whole(shape):
        return pl.BlockSpec(shape, lambda i: (0,) * len(shape))

    return pl.pallas_call(
        grid_kernel,
        grid=(PIECES // PSTEP,),
        in_specs=[
            pl.BlockSpec((1,), lambda i: (0,), memory_space=pltpu.SMEM),
            whole((128, 16, 128)),
            whole((2 * MW, PIECE)),
            whole((PIECES, 1, MW)),
            whole((PIECES, 1, MW)),
            whole((8, MW)),
        ],
        out_specs=pl.BlockSpec((PSTEP, SENT, 128), lambda i: (i, 0, 0)),
        out_shape=jax.ShapeDtypeStruct((PIECES, SENT, 128), BF16),
        scratch_shapes=[
            pltpu.VMEM((96, MW), F32),
            pltpu.VMEM((96, MW), F32),
            pltpu.VMEM((96 * PSTEP, 2 * MW), BF16),
        ],
        compiler_params=pltpu.CompilerParams(vmem_limit_bytes=48 * 1024 * 1024),
        name="grid_product",
    )(count, data, *tables)


def unpack_kernel(rows, out_u, out_v, out_t, wide):
    step = pl.program_id(0)
    for part in range(2):

        @pl.when(step == part)
        def _(part=part):
            for slot in range(BAND_MAX):
                chunk = rows[slot, 96 * part : 96 * part + 96]
                wide[97 * slot : 97 * slot + 96, :] = chunk.astype(F32)

    @pl.when(step == 2)
    def _():
        left = lax.broadcasted_iota(jnp.int32, (48, 128), 1) < 64
        pick_row = lax.broadcasted_iota(jnp.int32, (8, 128), 0) == 0
        pick_col = lax.broadcasted_iota(jnp.int32, (8, 128), 1) == 64
        pick = (pick_row & pick_col).astype(F32).astype(BF16)
        for slot in range(BAND_MAX):
            both = rows[slot, 192:240].astype(F32)
            last = lax.dot_general(
                rows[slot, 240:SENT], pick, (((0,), (0,)), ((), ())), preferred_element_type=F32
            )
            for half, val in enumerate((both, pltpu.roll(both, 64, 1))):
                val = jnp.where(left, val, 0.0) + last[48 * half : 48 * half + 48]
                wide[97 * slot + 48 * half : 97 * slot + 48 * half + 48, :] = val

    for lv in range(2):
        for fld, out in enumerate((out_u, out_v, out_t)):
            for src in range(16):
                row = lv * 48 + fld * 16 + src
                out[2 * src + lv] = wide[pl.ds(row, BAND_MAX, stride=97), :]


def unpack(rows):
    leaf = jax.ShapeDtypeStruct((LEVELS, BAND_MAX, PIECE), F32)
    return pl.pallas_call(
        unpack_kernel,
        grid=(PIECE // 128,),
        in_specs=[pl.BlockSpec((BAND_MAX, SENT, 128), lambda i: (0, 0, 0))],
        out_specs=[pl.BlockSpec((LEVELS, BAND_MAX, 128), lambda i: (0, 0, i))] * 3,
        out_shape=[leaf] * 3,
        scratch_shapes=[pltpu.VMEM((BAND_MAX * 97, 128), F32)],
        compiler_params=pltpu.CompilerParams(vmem_limit_bytes=24 * 1024 * 1024),
        name="unpack",
    )(rows)


def wave_row(orders):
    lower = orders[:, 0::2]
    both = jnp.stack([lower, MW - 1 - lower], axis=1)
    return jnp.concatenate([both[:, :, :KM].reshape(1, -1), both[:, :, KM:].reshape(1, -1)], axis=1)


def per_device(rot, dil, tmp, pol, orders, counts, limits):
    band = lax.axis_index("aa").astype(jnp.int32)
    slot = lax.axis_index("ba").astype(jnp.int32)
    sent = wind_legendre(rot, dil, tmp, pol, orders, limits, band[None])
    got = lax.all_to_all(sent, ("aa", "ba"), split_axis=0, concat_axis=0, tiled=True)
    edges = lax.dynamic_slice_in_dim(limits, band, 2, 0)
    lat = edges[0] + slot
    count = jnp.where(lat < edges[1], jnp.sum(jnp.where(jnp.arange(96) == lat, counts, 0)), 0)
    count = count.astype(jnp.int32)[None]
    tables = make_table(count, wave_row(orders))
    pieces = make_grid(count, got, tables)
    rows = lax.all_to_all(pieces, "ba", split_axis=0, concat_axis=0, tiled=True)
    return tuple(unpack(rows))


def solution(mesh):
    return jax.shard_map(
        per_device,
        mesh=mesh,
        in_specs=(
            P("ba", None, "aa"),
            P("ba", None, "aa"),
            P("ba", None, "aa"),
            P(None, "aa"),
            P(),
            P(),
            P(),
        ),
        out_specs=(P(None, "aa", "ba"), P(None, "aa", "ba"), P(None, "aa", "ba")),
        check_vma=False,
    )
```
